32 devices in a mesh: gx: 8 (over y, x, core), gy: 4 (over z).
Axes of the slice: x: 2, y: 2, z: 4, core: 2. Of those that a mesh axis runs over, the one named last changes fastest.
Arguments:
- tracers: float32 [96, 256, 2, 128], P('gx', 'gy'), may hold values from -6 to 6
- weights: float32 [96, 256, 48], P('gx', 'gy'), may hold values from 0 to 0.5
- offsets: int32 [96, 256, 4], P('gx', 'gy'), may hold values from -2 to 1
- owner: int32 [2, 8], replicated, may hold values from 0 to 7, as said below
- codes: int32 [2, 8], replicated, may hold values from 0 to 3
Outputs:
- updated: float32 [96, 256, 2, 128], P('gx', 'gy')
The draws below stay inside these ranges and needn't reach their ends.
Inputs may be any that keep to these rules, and one draw needn't show every extreme that they name: owner[0, b] names the column block whose first three rows are glued below block b, owner[1, b] the one whose last three rows are glued above it; each row of owner is a permutation of the 8 blocks, so every block's edge rows are glued to exactly one block on each side. `codes`: bit 0 reverses the glued rows along the columns, bit 1 reverses their order.
All inputs are finite; a program needn't handle non-finite values.
Results may differ from the reference program's by a relative error of at most 0.0003.
Values sent between devices are 32-bit elements; how exact they have to be, the bound alone decides.
No kernel may reach another device: no remote copies, remote signals or barrier semaphores. Data moves between devices by JAX's collectives and lax.ppermute only.
A program may use at most 128 MiB of HBM per device.

```python
import jax
import jax.numpy as jnp
from jax import lax

CX = 12
LEV = 2
Q = 128
BLOCKS = 8
NX = 96
NY = 256
N_GX = 8


def draw_owner(key, part):
    lower_perm = jax.random.permutation(jax.random.fold_in(key, 11), BLOCKS).astype(jnp.int32)
    upper_perm = jax.random.permutation(jax.random.fold_in(key, 23), BLOCKS).astype(jnp.int32)
    return jnp.stack([lower_perm, upper_perm], axis=0)


def plant(array, own_key, smallest, largest):
    spot = [jax.random.randint(jax.random.fold_in(own_key, axis), (), 0, length) for axis, length in enumerate(array.shape)]
    widest = array.shape.index(max(array.shape))
    neighbour = spot[:widest] + [(spot[widest] + 1) % array.shape[widest]] + spot[widest + 1:]
    return array.at[tuple(spot)].set(smallest).at[tuple(neighbour)].set(largest)


def steps_of(key, shape, pieces, least, top_value):
    def one(axis_at, parts):
        steps = jax.random.uniform(jax.random.fold_in(jax.random.fold_in(key, 6), axis_at), (parts,), jnp.float32, least / len(pieces), top_value / len(pieces))
        return jnp.repeat(jnp.exp(steps), shape[axis_at] // parts).reshape((-1,) + (1,) * (len(shape) - axis_at - 1))

    factor_of = one(*pieces[0])
    for cut in pieces[1:]:
        factor_of = factor_of * one(*cut)
    return factor_of


def centred(rng, dims, scale, reach, cuts=(), kind=jnp.bfloat16):
    gain = steps_of(rng, dims, cuts, -0.22, 0.18) if cuts else 1.0
    array = jax.random.normal(rng, dims, jnp.float32) * scale * gain
    return jnp.minimum(jnp.maximum(array, -reach), reach).astype(kind)


def setup_inputs(seed: int = 0) -> dict:
    keys = jax.random.split(jax.random.key(seed), 6)
    return {
        "tracers": centred(keys[0], (NX, NY, LEV, Q), 1.0, 6.0, ((0, 8), (1, 4)), jnp.float32),
        "weights": jnp.clip(0.5 * jax.random.uniform(keys[1], (NX, NY, LEV * 24), jnp.float32) ** steps_of(keys[1], (NX, NY, LEV * 24), ((0, 8), (1, 4)), -0.2, 0.2), 0.0, 0.5),
        "offsets": plant(jax.random.randint(keys[2], (NX, NY, LEV * 2), -2, 2), jax.random.fold_in(keys[2], 1), -2, 1).astype(jnp.int32),
        "owner": draw_owner(jax.random.fold_in(keys[5], 71), 0),
        "codes": plant(jax.random.randint(keys[4], (2, BLOCKS), 0, 4), jax.random.fold_in(keys[4], 1), 0, 3).astype(jnp.int32),
    }


def moment_list(extended):
    centre = extended[1:-1, 1:-1]
    east_side = extended[2:, 1:-1]
    west_side = extended[:-2, 1:-1]
    north_side = extended[1:-1, 2:]
    south_side = extended[1:-1, :-2]
    slope_east = 0.5 * (east_side - west_side)
    slope_north = 0.5 * (north_side - south_side)
    curve_east = 0.5 * (east_side - 2.0 * centre + west_side)
    curve_north = 0.5 * (north_side - 2.0 * centre + south_side)
    twist_both = 0.25 * (extended[2:, 2:] - extended[2:, :-2] - extended[:-2, 2:] + extended[:-2, :-2])
    return [centre, slope_east, slope_north, curve_east, curve_north, twist_both]


def remap_block(extended, weights, offsets):
    cols_out, rows_out = weights.shape[0], weights.shape[1]
    levels = offsets.shape[2] // 2
    tracer_count = extended.shape[3]
    moments = moment_list(extended)
    cols_mom, rows_mom = moments[0].shape[0], moments[0].shape[1]
    grid_cols = jnp.arange(cols_out, dtype=jnp.int32)[:, None]
    grid_rows = jnp.arange(rows_out, dtype=jnp.int32)[None, :]
    results = []
    for level_index in range(levels):
        moment_rows = jnp.stack([moment[:, :, level_index, :] for moment in moments], axis=2)
        moment_rows = moment_rows.reshape(cols_mom * rows_mom, 6 * tracer_count)
        summed = jnp.zeros((cols_out * rows_out, tracer_count), jnp.float32)
        for piece_index in range(4):
            step_col = piece_index // 2
            step_row = piece_index % 2
            source_col = grid_cols + offsets[:, :, 2 * level_index] + (step_col + 2)
            source_row = grid_rows + offsets[:, :, 2 * level_index + 1] + (step_row + 2)
            flat_index = (source_col * rows_mom + source_row).reshape(-1).astype(jnp.int32)
            gathered = jnp.take(moment_rows, flat_index, axis=0).reshape(-1, 6, tracer_count)
            first_weight = level_index * 24 + piece_index * 6
            piece_weights = weights[:, :, first_weight:first_weight + 6].reshape(-1, 6)
            summed = summed + jnp.einsum("ck,ckq->cq", piece_weights, gathered, precision=lax.Precision.HIGHEST)
        results.append(summed.reshape(cols_out, rows_out, tracer_count))
    return jnp.stack(results, axis=2)


def glued_strip(tracers, owner, codes, side_index, block_index):
    source_block = owner[side_index, block_index]
    code_value = codes[side_index, block_index]
    strip_cols = (source_block * CX - 3 + jnp.arange(CX + 6, dtype=jnp.int32)) % NX
    first_row = 0 if side_index == 0 else NY - 3
    strip_rows = jnp.take(tracers[:, first_row:first_row + 3], strip_cols.astype(jnp.int32), axis=0)
    strip_rows = jnp.where(code_value % 2 == 1, strip_rows[::-1], strip_rows)
    return jnp.where((code_value // 2) % 2 == 1, strip_rows[:, ::-1], strip_rows)


def reference(tracers, weights, offsets, owner, codes):
    def one_block(block_index):
        block_cols = (block_index * CX - 3 + jnp.arange(CX + 6, dtype=jnp.int32)) % NX
        middle = jnp.take(tracers, block_cols.astype(jnp.int32), axis=0)
        below = glued_strip(tracers, owner, codes, 0, block_index)
        above = glued_strip(tracers, owner, codes, 1, block_index)
        extended = jnp.concatenate([below, middle, above], axis=1)
        first_col = (block_index * CX).astype(jnp.int32)
        block_weights = lax.dynamic_slice_in_dim(weights, first_col, CX, 0)
        block_offsets = lax.dynamic_slice_in_dim(offsets, first_col, CX, 0)
        return remap_block(extended, block_weights, block_offsets)

    blocks = lax.map(one_block, jnp.arange(N_GX, dtype=jnp.int32))
    return blocks.reshape(NX, NY, LEV, Q)
```

```python
import functools

import jax
import jax.numpy as jnp
import numpy as np
from jax import lax
from jax.experimental import pallas as pl
from jax.experimental.pallas import tpu as pltpu
from jax.sharding import PartitionSpec as P

HALO = 3
BLOCK_X = 4
BLOCK_Y = 16
PITCH = 24
LANES = 128
LEAD = 4
BF16 = jnp.bfloat16
F32 = jnp.float32

STENCILS = [
    {(0, 0): 1.0},
    {(1, 0): 0.5, (-1, 0): -0.5},
    {(0, 1): 0.5, (0, -1): -0.5},
    {(1, 0): 0.5, (0, 0): -1.0, (-1, 0): 0.5},
    {(0, 1): 0.5, (0, 0): -1.0, (0, -1): 0.5},
    {(1, 1): 0.25, (1, -1): -0.25, (-1, 1): -0.25, (-1, -1): 0.25},
]


def spread_matrix(levels):
    terms = 24 * levels
    rows = 2 * terms + 8 * pl.cdiv(2 * levels, 8)
    matrix = np.zeros((rows, 2 * levels * LANES), np.float32)
    for level in range(levels):
        for piece in range(4):
            for moment, stencil in enumerate(STENCILS):
                for (east, north), value in stencil.items():
                    lane = (piece // 2 + 1 + east) * PITCH + piece % 2 + 1 + north
                    row = 24 * level + 6 * piece + moment
                    matrix[row, level * LANES + lane] += value
                    matrix[terms + row, level * LANES + lane] += value
        first = (levels + level) * LANES
        matrix[2 * terms + 2 * level, first : first + LANES] = PITCH
        matrix[2 * terms + 2 * level + 1, first : first + LANES] = 1
    return matrix


def band_kernel(levels, rows, weights_ref, offsets_ref, matrix_ref, band_ref):
    y_blocks = rows // BLOCK_Y
    lane = lax.broadcasted_iota(jnp.int32, (rows, LANES), 1)
    row_in = lax.broadcasted_iota(jnp.int32, (rows, LANES), 0) % BLOCK_Y
    base = lane - row_in - 2 * PITCH - 2
    pad = matrix_ref.shape[0] - 2 * weights_ref.shape[1] - offsets_ref.shape[1]

    def column(x, carry):
        weights = weights_ref[x]
        high = weights.astype(BF16).astype(F32)
        stacked = jnp.concatenate(
            [high, weights - high, offsets_ref[x].astype(F32), jnp.zeros((pad, rows), F32)], axis=0
        ).astype(BF16)
        spread = lax.dot_general(
            stacked, matrix_ref[...], (((0,), (0,)), ((), ())), preferred_element_type=F32
        )
        block, inner = x // BLOCK_X, x % BLOCK_X
        for level in range(levels):
            points = spread[:, level * LANES : (level + 1) * LANES]
            first = (levels + level) * LANES
            shift = spread[:, first : first + LANES].astype(jnp.int32)
            index = base - shift - inner * PITCH
            for part in range(2):
                here = index + part * LANES
                picked = jnp.take_along_axis(
                    points, here & (LANES - 1), axis=1, mode="promise_in_bounds"
                )
                band = jnp.where((here & ~(LANES - 1)) == 0, picked, 0.0)
                top = band.astype(BF16)
                rest = (band - top.astype(F32)).astype(BF16)
                for y in range(y_blocks):
                    slot = (block * y_blocks + y) * levels + level
                    at = pl.multiple_of(inner * BLOCK_Y, BLOCK_Y)
                    lanes = slice(part * LANES, (part + 1) * LANES)
                    mine = slice(y * BLOCK_Y, (y + 1) * BLOCK_Y)
                    band_ref[slot, pl.ds(at, BLOCK_Y), lanes] = top[mine]
                    low = pl.multiple_of(at + BLOCK_X * BLOCK_Y, BLOCK_Y)
                    band_ref[slot, pl.ds(low, BLOCK_Y), lanes] = rest[mine]
        return carry

    lax.fori_loop(0, weights_ref.shape[0], column, 0)


def pack_kernel(cells_ref, edges_ref, inner_ref, outer_ref):
    cols, rows, _ = cells_ref.shape
    width = edges_ref.shape[0] // cols // 2
    even = lax.axis_index("gx") % 2 == 0
    for col in range(cols):
        at = 2 * width * col
        edges_ref[at : at + width] = cells_ref[col, :width]
        edges_ref[at + width : at + 2 * width] = cells_ref[col, rows - width :]
    last = cols - HALO
    for col in range(HALO):
        to = slice(col * rows, (col + 1) * rows)
        inner_ref[to] = cells_ref[jnp.where(even, last + col, col)]
        outer_ref[to] = cells_ref[jnp.where(even, col, last + col)]


def strip_kernel(cols, width, edges_ref, other_ref, message_ref):
    even = lax.axis_index("gx") % 2 == 0
    low = lax.axis_index("gy") == 0
    for col in range(cols):
        at = 2 * width * col
        mine = jnp.where(low, edges_ref[at : at + width], edges_ref[at + width : at + 2 * width])
        theirs = jnp.where(low, other_ref[at : at + width], other_ref[at + width : at + 2 * width])
        message_ref[width * col : width * (col + 1)] = jnp.where(even, mine, theirs)
        to = width * (cols + col)
        message_ref[to : to + width] = jnp.where(even, theirs, mine)
    corner = 2 * width * HALO
    first, last = edges_ref[:corner], edges_ref[2 * width * cols - corner :]
    at = 2 * width * cols
    message_ref[at : at + corner] = jnp.where(even, first, last)
    end = message_ref.shape[0]
    if end > at + corner:
        message_ref[at + corner :] = jnp.zeros((end - at - corner, LANES), F32)


class Window:
    def __init__(self, cols, width, count, run, based, own, got):
        self.cols, self.width, self.total, self.run = cols, width, count * cols, run
        self.count, self.own, self.got = count, own, got
        index = lax.axis_index("gx")
        even = index % 2 == 0
        self.half = run * cols // 2
        self.own_low = jnp.logical_not(even) if based else None
        self.first = jnp.where(even, index - 2, index - 1)

    def start(self, owner):
        return lax.rem((owner - self.first) * self.cols - HALO + 2 * self.total, self.total)

    def column(self, start, step):
        at = start + step
        at = jnp.where(at >= self.total, at - self.total, at)
        held = at < self.run * self.cols
        at = jnp.minimum(at, self.run * self.cols - 1)
        low = at < self.half
        row = jnp.where(low, at, at - self.half) * self.width
        own, got = self.own[pl.ds(row, self.width)], self.got[pl.ds(row, self.width)]
        from_own = low if self.own_low is None else low == self.own_low
        return held, jnp.where(from_own, own, got)


def rows_kernel(cols, width, count, ends, run, based, owner_ref, edges_ref, other_ref, got_ref,
                own_run_ref, got_run_ref, first_ref, second_ref):
    index, place = lax.axis_index("gx"), lax.axis_index("gy")
    even = index % 2 == 0
    flat_place = place % 2 == 0
    corner = 2 * width * cols

    def rows(ref, at, top):
        return jnp.where(top, ref[at + width : at + 2 * width], ref[at : at + width])

    def column(u, top):
        if u < HALO:
            near = rows(other_ref, 2 * width * (cols - HALO + u), top)
            far = rows(got_ref, corner + 2 * width * u, top)
            return jnp.where(even, far, near)
        if u < HALO + cols:
            return rows(edges_ref, 2 * width * (u - HALO), top)
        near = rows(other_ref, 2 * width * (u - HALO - cols), top)
        far = rows(got_ref, corner + 2 * width * (u - HALO - cols), top)
        return jnp.where(even, near, far)

    wide = cols + 2 * HALO
    window = Window(cols, width, count, run, based, own_run_ref, got_run_ref)
    side = jnp.where(place == 0, 0, 1)
    target = lax.rem(index + count // 2, count)
    start = window.start(owner_ref[side, target])
    is_end = jnp.logical_or(place == 0, place == ends - 1)
    for u in range(wide):
        to = slice(u * width, (u + 1) * width)
        first_ref[to] = column(u, flat_place)
        _, glued = window.column(start, u)
        second_ref[to] = jnp.where(is_end, glued, column(u, jnp.logical_not(flat_place)))
    end = first_ref.shape[0]
    if end > wide * width:
        first_ref[wide * width :] = jnp.zeros((end - wide * width, LANES), F32)
        second_ref[wide * width :] = jnp.zeros((end - wide * width, LANES), F32)


def remap_kernel(levels, count, ends, run, based, owner_ref, codes_ref, cells_ref, inner_ref,
                 outer_ref, first_ref, second_ref, own_run_ref, got_run_ref, band_ref, out_ref,
                 field_ref):
    cols, rows, _ = cells_ref.shape
    width = HALO * levels
    lead = LEAD * levels
    index, place = lax.axis_index("gx"), lax.axis_index("gy")
    even = index % 2 == 0
    flat_place = place % 2 == 0
    wide = cols + 2 * HALO

    for col in range(cols):
        field_ref[HALO + col, lead : lead + rows] = cells_ref[col]
    for col in range(HALO):
        inner = inner_ref[col * rows : (col + 1) * rows]
        outer = outer_ref[col * rows : (col + 1) * rows]
        field_ref[col, lead : lead + rows] = jnp.where(even, outer, inner)
        field_ref[HALO + cols + col, lead : lead + rows] = jnp.where(even, inner, outer)

    window = Window(cols, width, count, run, based, own_run_ref, got_run_ref)
    side = jnp.where(place == 0, 0, 1)
    code = codes_ref[side, index]
    start = window.start(owner_ref[side, index])
    is_end = jnp.logical_or(place == 0, place == ends - 1)
    mirrored = jnp.logical_and(is_end, code % 2 == 1)
    flipped = jnp.logical_and(is_end, code // 2 % 2 == 1)
    tail = field_ref.shape[1] - lead - rows - width
    for u in range(wide):
        plain = first_ref[u * width : (u + 1) * width]
        step = jnp.where(mirrored, wide - 1 - u, u)
        held, glued = window.column(start, step)
        come = second_ref[pl.ds(step * width, width)]
        strip = jnp.where(jnp.logical_and(is_end, held), glued, come)
        turned = jnp.concatenate(
            [strip[levels * r : levels * (r + 1)] for r in reversed(range(HALO))], axis=0
        )
        strip = jnp.where(flipped, turned, strip)
        field_ref[u, lead - width : lead] = jnp.where(flat_place, strip, plain)
        field_ref[u, lead + rows : lead + rows + width] = jnp.where(flat_place, plain, strip)
        field_ref[u, lead + rows + width :] = jnp.zeros((tail, LANES), F32)

    x_blocks, y_blocks = cols // BLOCK_X, rows // levels // BLOCK_Y
    size = BLOCK_X * BLOCK_Y
    reach = BLOCK_X + 2 * HALO
    spare = jnp.zeros((2 * LANES - reach * PITCH, LANES), F32)

    def block_row(step, carry):
        y, level = step // levels, step % levels
        begin = (y * BLOCK_Y + LEAD - HALO) * levels + level
        for x in range(x_blocks):
            points = jnp.concatenate(
                [
                    field_ref[x * BLOCK_X + c, pl.ds(begin, PITCH, stride=levels), :]
                    for c in range(reach)
                ]
                + [spare],
                axis=0,
            )
            top = points.astype(BF16)
            rest = (points - top.astype(F32)).astype(BF16)
            band = band_ref[(x * y_blocks + y) * levels + level]
            product = jnp.dot(
                band, jnp.concatenate([top, rest], axis=1), preferred_element_type=F32
            )
            total = product[:size, :LANES] + (product[:size, LANES:] + product[size:, :LANES])
            for c in range(BLOCK_X):
                out_ref[
                    x * BLOCK_X + c, pl.ds(y * BLOCK_Y * levels + level, BLOCK_Y, stride=levels), :
                ] = total[c * BLOCK_Y : (c + 1) * BLOCK_Y]
        return carry

    lax.fori_loop(0, y_blocks * levels, block_row, 0)


VMEM = pl.BlockSpec(memory_space=pltpu.VMEM)
SMEM = pl.BlockSpec(memory_space=pltpu.SMEM)


def shaped(*shape, dtype=F32):
    return jax.ShapeDtypeStruct(shape, dtype)


def eights(rows):
    return 8 * pl.cdiv(rows, 8)


def on_device(tracers, weights, offsets, owner, codes, matrix):
    cols, rows, levels, lanes = tracers.shape
    width = HALO * levels
    count, ends = lax.axis_size("gx"), lax.axis_size("gy")
    axes = ("gx", "gy")
    cells = tracers.reshape(cols, rows * levels, lanes)
    partner = [(i, i ^ 1) for i in range(count)]
    across = [(i, (i + 1) % count if i % 2 else (i - 1) % count) for i in range(count)]
    first_swap = [(i * ends + j, i * ends + (j ^ 1)) for i in range(count) for j in range(ends)]
    second_swap = []
    for i in range(count):
        for j in range(ends):
            if j in (0, ends - 1):
                second_swap.append((i * ends + j, (i + count // 2) % count * ends + j))
            else:
                second_swap.append((i * ends + j, i * ends + (j + 1 if j % 2 else j - 1)))

    edges, inner, outer = pl.pallas_call(
        pack_kernel,
        out_shape=(
            shaped(2 * width * cols, lanes),
            shaped(HALO * rows * levels, lanes),
            shaped(HALO * rows * levels, lanes),
        ),
        in_specs=[VMEM],
        out_specs=(VMEM, VMEM, VMEM),
        name="pack",
    )(cells)
    other = lax.ppermute(edges, "gx", partner)
    inner_got = lax.ppermute(inner, "gx", partner)

    strip_rows = 2 * width * cols
    message = pl.pallas_call(
        functools.partial(strip_kernel, cols, width),
        out_shape=shaped(eights(strip_rows + 2 * width * HALO), lanes),
        in_specs=[VMEM, VMEM],
        out_specs=VMEM,
        name="strip",
    )(edges, other)
    got = lax.ppermute(message, "gx", across)
    outer_got = lax.ppermute(outer, "gx", across)

    run, based = 4, True
    own_run, got_run = message, got
    if count // 2 > run:
        mine, theirs = message[:strip_rows], got[:strip_rows]
        own_run = jnp.where(
            lax.axis_index("gx") % 2 == 0,
            jnp.concatenate([theirs, mine]),
            jnp.concatenate([mine, theirs]),
        )
        based = False
        while True:
            shift = run
            got_run = lax.ppermute(
                own_run, "gx", [((i + shift) % count, i) for i in range(count)]
            )
            run *= 2
            if run >= count // 2:
                break
            own_run = jnp.concatenate([own_run, got_run])

    z_rows = eights(width * (cols + 2 * HALO))
    first, second = pl.pallas_call(
        functools.partial(rows_kernel, cols, width, count, ends, run, based),
        out_shape=(shaped(z_rows, lanes), shaped(z_rows, lanes)),
        in_specs=[SMEM] + [VMEM] * 5,
        out_specs=(VMEM, VMEM),
        name="rows",
    )(owner, edges, other, got, own_run, got_run)
    first_got = lax.ppermute(first, axes, first_swap)
    second_got = lax.ppermute(second, axes, second_swap)

    slots = cols // BLOCK_X * (rows // BLOCK_Y) * levels
    band = pl.pallas_call(
        functools.partial(band_kernel, levels, rows),
        out_shape=shaped(slots, 2 * BLOCK_X * BLOCK_Y, 2 * LANES, dtype=BF16),
        in_specs=[VMEM] * 3,
        out_specs=VMEM,
        name="band",
        cost_estimate=pl.CostEstimate(
            flops=4 * 10**8, bytes_accessed=3 * 10**6, transcendentals=0
        ),
    )(jnp.swapaxes(weights, 1, 2), jnp.swapaxes(offsets, 1, 2), matrix)

    field_rows = eights((LEAD + rows + HALO + PITCH - BLOCK_Y - 2 * HALO) * levels)
    updated = pl.pallas_call(
        functools.partial(remap_kernel, levels, count, ends, run, based),
        out_shape=shaped(cols, rows * levels, lanes),
        in_specs=[SMEM, SMEM] + [VMEM] * 8,
        out_specs=VMEM,
        scratch_shapes=[pltpu.VMEM((cols + 2 * HALO, field_rows, lanes), F32)],
        name="remap",
    )(owner, codes, cells, inner_got, outer_got, first_got, second_got, own_run, got_run, band)
    return updated.reshape(cols, rows, levels, lanes)


def solution(mesh):
    split = P("gx", "gy", None, None)
    in_specs = (split, P("gx", "gy", None), P("gx", "gy", None), P(), P(), P())

    def run(tracers, weights, offsets, owner, codes):
        matrix = jnp.asarray(spread_matrix(tracers.shape[2]), BF16)
        body = jax.shard_map(
            on_device, mesh=mesh, in_specs=in_specs, out_specs=split, check_vma=False
        )
        return body(tracers, weights, offsets, owner, codes, matrix)

    return run
```

```python
import functools

import jax
import jax.numpy as jnp
import numpy as np
from jax import lax
from jax.experimental import pallas as pl
from jax.experimental.pallas import tpu as pltpu
from jax.sharding import PartitionSpec as P

HALO = 3
BLOCK_X = 4
BLOCK_Y = 16
PITCH = 24
LANES = 128
LEAD = 4
UNROLL = 4
BF16 = jnp.bfloat16
F32 = jnp.float32

STENCILS = [
    {(0, 0): 1.0},
    {(1, 0): 0.5, (-1, 0): -0.5},
    {(0, 1): 0.5, (0, -1): -0.5},
    {(1, 0): 0.5, (0, 0): -1.0, (-1, 0): 0.5},
    {(0, 1): 0.5, (0, 0): -1.0, (0, -1): 0.5},
    {(1, 1): 0.25, (1, -1): -0.25, (-1, 1): -0.25, (-1, -1): 0.25},
]


def spread_matrix(levels):
    terms = 24 * levels
    rows = 2 * terms + 8 * pl.cdiv(2 * levels, 8)
    matrix = np.zeros((rows, 2 * levels * LANES), np.float32)
    for level in range(levels):
        for piece in range(4):
            for moment, stencil in enumerate(STENCILS):
                for (east, north), value in stencil.items():
                    lane = (piece // 2 + 1 + east) * PITCH + piece % 2 + 1 + north
                    row = 24 * level + 6 * piece + moment
                    matrix[row, level * LANES + lane] += value
                    matrix[terms + row, level * LANES + lane] += value
        first = (levels + level) * LANES
        matrix[2 * terms + 2 * level, first : first + LANES] = PITCH
        matrix[2 * terms + 2 * level + 1, first : first + LANES] = 1
    return matrix


def columns_kernel(cells_ref, after_ref, inner_ref, outer_ref, sems):
    del after_ref
    even = lax.axis_index("gx") % 2 == 0
    last = cells_ref.shape[0] - HALO
    copies = [
        pltpu.make_async_copy(
            cells_ref.at[pl.ds(jnp.where(even, last, 0), HALO)], inner_ref, sems.at[0]
        ),
        pltpu.make_async_copy(
            cells_ref.at[pl.ds(jnp.where(even, 0, last), HALO)], outer_ref, sems.at[1]
        ),
    ]
    for copy in copies:
        copy.start()
    for copy in copies:
        copy.wait()


def band_kernel(levels, rows, count, ends, run, based, owner_ref, codes_ref, weights_hbm, offsets_hbm,
                matrix_hbm, after_ref, band_ref, table_ref, weights_ref, offsets_ref, matrix_ref, sems):
    del after_ref
    cols = weights_ref.shape[0]
    groups = cols // UNROLL

    def fetch(group):
        part = pl.ds(group * UNROLL, UNROLL)
        return pltpu.make_async_copy(weights_hbm.at[part], weights_ref.at[part], sems.at[group])

    others = [
        pltpu.make_async_copy(offsets_hbm, offsets_ref, sems.at[groups]),
        pltpu.make_async_copy(matrix_hbm, matrix_ref, sems.at[groups + 1]),
    ]
    fetch(0).start()
    for copy in others:
        copy.start()
    for group in range(1, groups):
        fetch(group).start()

    index, place = lax.axis_index("gx"), lax.axis_index("gy")
    side = jnp.where(place == 0, 0, 1)
    window = Window(cols, 0, count, run, based, None, None)
    target = lax.rem(index + count // 2, count)
    is_end = jnp.logical_or(place == 0, place == ends - 1)
    code = jnp.where(is_end, codes_ref[side, index], 0)
    lines = [window.start(owner_ref[side, target]), window.start(owner_ref[side, index]), code]
    for at, line in enumerate(lines):
        table_ref[at : at + 1] = jnp.full((1, LANES), line, jnp.int32)
    for copy in others:
        copy.wait()

    y_blocks = rows // BLOCK_Y
    lane = lax.broadcasted_iota(jnp.int32, (rows, LANES), 1)
    row_in = lax.broadcasted_iota(jnp.int32, (rows, LANES), 0) % BLOCK_Y
    base = lane - row_in - 2 * PITCH - 2
    pad = matrix_ref.shape[0] - 2 * weights_ref.shape[1] - offsets_ref.shape[1]

    def column(x):
        weights = weights_ref[x]
        high = weights.astype(BF16).astype(F32)
        stacked = jnp.concatenate(
            [high, weights - high, offsets_ref[x].astype(F32), jnp.zeros((pad, rows), F32)], axis=0
        ).astype(BF16)
        spread = lax.dot_general(
            stacked, matrix_ref[...], (((0,), (0,)), ((), ())), preferred_element_type=F32
        )
        block, inner = x // BLOCK_X, x % BLOCK_X
        at = pl.multiple_of(inner * BLOCK_Y, BLOCK_Y)
        low = pl.multiple_of(at + BLOCK_X * BLOCK_Y, BLOCK_Y)
        for level in range(levels):
            points = spread[:, level * LANES : (level + 1) * LANES]
            first = (levels + level) * LANES
            shift = spread[:, first : first + LANES].astype(jnp.int32)
            for y in range(y_blocks):
                mine = slice(y * BLOCK_Y, (y + 1) * BLOCK_Y)
                index = base[mine] - shift[mine] - inner * PITCH
                picked = jnp.take_along_axis(
                    points[mine], index & (LANES - 1), axis=1, mode="promise_in_bounds"
                )
                top = picked.astype(BF16).astype(F32)
                rest = picked - top
                here = index >= 0
                slot = (block * y_blocks + y) * levels + level
                for part in range(2):
                    lanes = slice(part * LANES, (part + 1) * LANES)
                    keep = here if part == 0 else jnp.logical_not(here)
                    band_ref[slot, pl.ds(at, BLOCK_Y), lanes] = jnp.where(keep, top, 0.0).astype(BF16)
                    band_ref[slot, pl.ds(low, BLOCK_Y), lanes] = jnp.where(keep, rest, 0.0).astype(BF16)

    def group_of(group, carry):
        fetch(group).wait()
        for step in range(UNROLL):
            column(group * UNROLL + step)
        return carry

    lax.fori_loop(0, groups, group_of, 0)


def pack_kernel(cells_ref, edges_ref, low_ref, high_ref, sems):
    cols, rows, _ = cells_ref.shape
    width = edges_ref.shape[0] // cols // 2
    deep = low_ref.shape[1]
    copies = [
        pltpu.make_async_copy(cells_ref.at[:, pl.ds(0, deep)], low_ref, sems.at[0]),
        pltpu.make_async_copy(cells_ref.at[:, pl.ds(rows - deep, deep)], high_ref, sems.at[1]),
    ]
    for copy in copies:
        copy.start()
    for copy in copies:
        copy.wait()
    for col in range(cols):
        at = 2 * width * col
        edges_ref[at : at + width] = low_ref[col, :width]
        edges_ref[at + width : at + 2 * width] = high_ref[col, deep - width :]


def strip_kernel(cols, width, edges_ref, other_ref, after_ref, message_ref):
    del after_ref
    even = lax.axis_index("gx") % 2 == 0
    low = lax.axis_index("gy") == 0
    for col in range(cols):
        at = 2 * width * col
        mine = jnp.where(low, edges_ref[at : at + width], edges_ref[at + width : at + 2 * width])
        theirs = jnp.where(low, other_ref[at : at + width], other_ref[at + width : at + 2 * width])
        message_ref[width * col : width * (col + 1)] = jnp.where(even, mine, theirs)
        to = width * (cols + col)
        message_ref[to : to + width] = jnp.where(even, theirs, mine)
    corner = 2 * width * HALO
    first, last = edges_ref[:corner], edges_ref[2 * width * cols - corner :]
    at = 2 * width * cols
    message_ref[at : at + corner] = jnp.where(even, first, last)
    end = message_ref.shape[0]
    if end > at + corner:
        message_ref[at + corner :] = jnp.zeros((end - at - corner, LANES), F32)


class Window:
    def __init__(self, cols, width, count, run, based, own, got):
        self.cols, self.width, self.total, self.run = cols, width, count * cols, run
        self.count, self.own, self.got = count, own, got
        index = lax.axis_index("gx")
        even = index % 2 == 0
        self.half = run * cols // 2
        self.own_low = jnp.logical_not(even) if based else None
        self.first = jnp.where(even, index - 2, index - 1)

    def start(self, owner):
        return lax.rem((owner - self.first) * self.cols - HALO + 2 * self.total, self.total)

    def column(self, start, step):
        at = start + step
        at = jnp.where(at >= self.total, at - self.total, at)
        held = at < self.run * self.cols
        at = jnp.minimum(at, self.run * self.cols - 1)
        low = at < self.half
        row = jnp.where(low, at, at - self.half) * self.width
        own, got = self.own[pl.ds(row, self.width)], self.got[pl.ds(row, self.width)]
        from_own = low if self.own_low is None else low == self.own_low
        return held, jnp.where(from_own, own, got)


def rows_kernel(cols, width, count, ends, run, based, table_ref, edges_ref, other_ref, got_ref,
                own_run_ref, got_run_ref, after_ref, first_ref, second_ref):
    del after_ref
    even, place = lax.axis_index("gx") % 2 == 0, lax.axis_index("gy")
    flat_place = place % 2 == 0
    corner = 2 * width * cols

    def rows(ref, at, top):
        return jnp.where(top, ref[at + width : at + 2 * width], ref[at : at + width])

    def column(u, top):
        if u < HALO:
            near = rows(other_ref, 2 * width * (cols - HALO + u), top)
            far = rows(got_ref, corner + 2 * width * u, top)
            return jnp.where(even, far, near)
        if u < HALO + cols:
            return rows(edges_ref, 2 * width * (u - HALO), top)
        near = rows(other_ref, 2 * width * (u - HALO - cols), top)
        far = rows(got_ref, corner + 2 * width * (u - HALO - cols), top)
        return jnp.where(even, near, far)

    wide = cols + 2 * HALO
    window = Window(cols, width, count, run, based, own_run_ref, got_run_ref)
    start = table_ref[0:1, 0:1][0, 0]
    is_end = jnp.logical_or(place == 0, place == ends - 1)
    for u in range(wide):
        to = slice(u * width, (u + 1) * width)
        first_ref[to] = column(u, flat_place)
        _, glued = window.column(start, u)
        second_ref[to] = jnp.where(is_end, glued, column(u, jnp.logical_not(flat_place)))
    end = first_ref.shape[0]
    if end > wide * width:
        first_ref[wide * width :] = jnp.zeros((end - wide * width, LANES), F32)
        second_ref[wide * width :] = jnp.zeros((end - wide * width, LANES), F32)


def block_sum(field_ref, band_ref, x, y, y_blocks, levels, level):
    size = BLOCK_X * BLOCK_Y
    reach = BLOCK_X + 2 * HALO
    begin = (y * BLOCK_Y + LEAD - HALO) * levels + level
    points = jnp.concatenate(
        [
            field_ref[x * BLOCK_X + c, pl.ds(begin, PITCH, stride=levels), :]
            for c in range(reach)
        ]
        + [jnp.zeros((2 * LANES - reach * PITCH, LANES), F32)],
        axis=0,
    )
    top = points.astype(BF16)
    rest = (points - top.astype(F32)).astype(BF16)
    band = band_ref[(x * y_blocks + y) * levels + level]
    product = jnp.dot(band, jnp.concatenate([top, rest], axis=1), preferred_element_type=F32)
    return product[:size, :LANES] + (product[:size, LANES:] + product[size:, :LANES])


def remap_rows(field_ref, band_ref, stage_ref, out_ref, sems, levels, y_blocks, which):
    x_blocks = stage_ref.shape[1] // BLOCK_X
    deep = BLOCK_Y * levels
    copies = []
    for at, y in enumerate(which):
        for level in range(levels):
            for x in range(x_blocks):
                total = block_sum(field_ref, band_ref, x, y, y_blocks, levels, level)
                for c in range(BLOCK_X):
                    stage_ref[at, x * BLOCK_X + c, pl.ds(level, BLOCK_Y, stride=levels), :] = total[
                        c * BLOCK_Y : (c + 1) * BLOCK_Y
                    ]
        copies.append(
            pltpu.make_async_copy(
                stage_ref.at[at], out_ref.at[:, pl.ds(y * deep, deep)], sems.at[at]
            )
        )
        copies[-1].start()
    for copy in copies:
        copy.wait()


def middle_kernel(levels, cells_ref, inner_ref, outer_ref, band_ref, after_ref, out_ref, field_ref,
                  stage_ref, sems):
    del after_ref
    cols, rows, _ = cells_ref.shape
    lead = LEAD * levels
    even = lax.axis_index("gx") % 2 == 0
    for col in range(cols):
        field_ref[HALO + col, lead : lead + rows] = cells_ref[col]
    for col in range(HALO):
        inner, outer = inner_ref[col], outer_ref[col]
        field_ref[col, lead : lead + rows] = jnp.where(even, outer, inner)
        field_ref[HALO + cols + col, lead : lead + rows] = jnp.where(even, inner, outer)
    y_blocks = rows // levels // BLOCK_Y
    remap_rows(
        field_ref, band_ref, stage_ref, out_ref, sems, levels, y_blocks, range(1, y_blocks - 1)
    )


def edge_kernel(levels, cols, rows, count, ends, run, based, table_ref, first_ref, second_ref,
                own_run_ref, got_run_ref, band_ref, field_in, out_in, field_ref, out_ref,
                stage_ref, sems):
    del field_in, out_in
    width = HALO * levels
    lead = LEAD * levels
    place = lax.axis_index("gy")
    flat_place = place % 2 == 0
    wide = cols + 2 * HALO
    window = Window(cols, width, count, run, based, own_run_ref, got_run_ref)
    start, code = table_ref[1:2, 0:1][0, 0], table_ref[2:3, 0:1][0, 0]
    is_end = jnp.logical_or(place == 0, place == ends - 1)
    mirrored = code % 2 == 1
    flipped = code // 2 % 2 == 1
    tail = field_ref.shape[1] - lead - rows - width
    for u in range(wide):
        plain = first_ref[u * width : (u + 1) * width]
        step = jnp.where(mirrored, wide - 1 - u, u)
        held, glued = window.column(start, step)
        come = second_ref[pl.ds(step * width, width)]
        strip = jnp.where(jnp.logical_and(is_end, held), glued, come)
        turned = jnp.concatenate(
            [strip[levels * r : levels * (r + 1)] for r in reversed(range(HALO))], axis=0
        )
        strip = jnp.where(flipped, turned, strip)
        field_ref[u, lead - width : lead] = jnp.where(flat_place, strip, plain)
        field_ref[u, lead + rows : lead + rows + width] = jnp.where(flat_place, plain, strip)
        field_ref[u, lead + rows + width :] = jnp.zeros((tail, LANES), F32)
    y_blocks = rows // levels // BLOCK_Y
    remap_rows(
        field_ref, band_ref, stage_ref, out_ref, sems, levels, y_blocks, (0, y_blocks - 1)
    )


def grant(mebibytes):
    return pltpu.CompilerParams(vmem_limit_bytes=mebibytes << 20)


def takes(microseconds):
    return pl.CostEstimate(
        flops=0, bytes_accessed=int(microseconds * 3_000_000), transcendentals=0
    )


def in_hbm(array):
    return pltpu.with_memory_space_constraint(array, pltpu.HBM)


VMEM = pl.BlockSpec(memory_space=pltpu.VMEM)
HBM = pl.BlockSpec(memory_space=pltpu.HBM)
ANY = pl.BlockSpec(memory_space=pl.ANY)
SMEM = pl.BlockSpec(memory_space=pltpu.SMEM)


def shaped(*shape, dtype=F32):
    return jax.ShapeDtypeStruct(shape, dtype)


def eights(rows):
    return 8 * pl.cdiv(rows, 8)


def on_device(tracers, weights, offsets, owner, codes, matrix):
    cols, rows, levels, lanes = tracers.shape
    width = HALO * levels
    count, ends = lax.axis_size("gx"), lax.axis_size("gy")
    axes = ("gx", "gy")
    cells = tracers.reshape(cols, rows * levels, lanes)
    partner = [(i, i ^ 1) for i in range(count)]
    across = [(i, (i + 1) % count if i % 2 else (i - 1) % count) for i in range(count)]
    first_swap = [(i * ends + j, i * ends + (j ^ 1)) for i in range(count) for j in range(ends)]
    second_swap = []
    for i in range(count):
        for j in range(ends):
            if j in (0, ends - 1):
                second_swap.append((i * ends + j, (i + count // 2) % count * ends + j))
            else:
                second_swap.append((i * ends + j, i * ends + (j + 1 if j % 2 else j - 1)))

    deep = eights(width)
    edges = pl.pallas_call(
        pack_kernel,
        out_shape=shaped(2 * width * cols, lanes),
        in_specs=[HBM],
        out_specs=VMEM,
        scratch_shapes=[
            pltpu.VMEM((cols, deep, lanes), F32),
            pltpu.VMEM((cols, deep, lanes), F32),
            pltpu.SemaphoreType.DMA((2,)),
        ],
        name="pack",
        compiler_params=grant(4),
        cost_estimate=takes(1.0),
    )(in_hbm(cells))
    other = lax.ppermute(edges, "gx", partner)

    columns = shaped(HALO, rows * levels, lanes)
    inner, outer = pl.pallas_call(
        columns_kernel,
        out_shape=(columns, columns),
        in_specs=[HBM, ANY],
        out_specs=(VMEM, VMEM),
        scratch_shapes=[pltpu.SemaphoreType.DMA((2,))],
        name="columns",
        compiler_params=grant(4),
        cost_estimate=takes(0.5),
    )(in_hbm(cells), edges)

    strip_rows = 2 * width * cols
    message = pl.pallas_call(
        functools.partial(strip_kernel, cols, width),
        out_shape=shaped(eights(strip_rows + 2 * width * HALO), lanes),
        in_specs=[VMEM, VMEM, ANY],
        out_specs=VMEM,
        name="strip",
        cost_estimate=takes(1.0),
        compiler_params=grant(4),
    )(edges, other, inner)
    got = lax.ppermute(message, "gx", across)
    outer_got = lax.ppermute(outer, "gx", across)
    inner_got = lax.ppermute(inner, "gx", partner)

    run, based = 4, True
    own_run, got_run = message, got
    if count // 2 > run:
        mine, theirs = message[:strip_rows], got[:strip_rows]
        own_run = jnp.where(
            lax.axis_index("gx") % 2 == 0,
            jnp.concatenate([theirs, mine]),
            jnp.concatenate([mine, theirs]),
        )
        based = False
        while True:
            shift = run
            got_run = lax.ppermute(
                own_run, "gx", [((i + shift) % count, i) for i in range(count)]
            )
            run *= 2
            if run >= count // 2:
                break
            own_run = jnp.concatenate([own_run, got_run])

    weights = jnp.swapaxes(weights, 1, 2)
    offsets = jnp.swapaxes(offsets, 1, 2)
    y_blocks = rows // BLOCK_Y
    slots = cols // BLOCK_X * y_blocks * levels
    band, table = pl.pallas_call(
        functools.partial(band_kernel, levels, rows, count, ends, run, based),
        out_shape=(
            shaped(slots, 2 * BLOCK_X * BLOCK_Y, 2 * LANES, dtype=BF16),
            shaped(8, lanes, dtype=jnp.int32),
        ),
        in_specs=[SMEM, SMEM] + [HBM] * 3 + [ANY],
        out_specs=(VMEM, VMEM),
        scratch_shapes=[
            pltpu.VMEM(weights.shape, F32),
            pltpu.VMEM(offsets.shape, jnp.int32),
            pltpu.VMEM(matrix.shape, BF16),
            pltpu.SemaphoreType.DMA((cols // UNROLL + 2,)),
        ],
        name="band",
        compiler_params=grant(6),
        cost_estimate=takes(3.0),
    )(*[in_hbm(a) for a in (owner, codes, weights, offsets, matrix)], message)

    z_rows = eights(width * (cols + 2 * HALO))
    first, second = pl.pallas_call(
        functools.partial(rows_kernel, cols, width, count, ends, run, based),
        out_shape=(shaped(z_rows, lanes), shaped(z_rows, lanes)),
        in_specs=[VMEM] * 6 + [ANY],
        out_specs=(VMEM, VMEM),
        name="rows",
        cost_estimate=takes(1.0),
        compiler_params=grant(2),
    )(table, edges, other, got, own_run, got_run, band)
    first_got = lax.ppermute(first, axes, first_swap)
    second_got = lax.ppermute(second, axes, second_swap)

    field_rows = eights((LEAD + rows + HALO + PITCH - BLOCK_Y - 2 * HALO) * levels)
    field_shape = shaped(cols + 2 * HALO, field_rows, lanes)
    out_shape = shaped(cols, rows * levels, lanes)
    stage = (cols, BLOCK_Y * levels, lanes)
    partial, field = pl.pallas_call(
        functools.partial(middle_kernel, levels),
        out_shape=(out_shape, field_shape),
        in_specs=[VMEM] * 4 + [ANY],
        out_specs=(HBM, VMEM),
        scratch_shapes=[
            pltpu.VMEM((y_blocks - 2, *stage), F32),
            pltpu.SemaphoreType.DMA((y_blocks - 2,)),
        ],
        name="middle",
        cost_estimate=takes(2.0),
        compiler_params=grant(6),
    )(cells, inner_got, outer_got, band, first)
    _, updated = pl.pallas_call(
        functools.partial(edge_kernel, levels, cols, rows * levels, count, ends, run, based),
        out_shape=(field_shape, out_shape),
        in_specs=[VMEM] * 7 + [HBM],
        out_specs=(VMEM, HBM),
        scratch_shapes=[pltpu.VMEM((2, *stage), F32), pltpu.SemaphoreType.DMA((2,))],
        input_output_aliases={6: 0, 7: 1},
        name="edge",
        cost_estimate=takes(2.0),
        compiler_params=grant(6),
    )(table, first_got, second_got, own_run, got_run, band, field, partial)
    return updated.reshape(cols, rows, levels, lanes)


def solution(mesh):
    split = P("gx", "gy", None, None)
    in_specs = (split, P("gx", "gy", None), P("gx", "gy", None), P(), P(), P())


    def run(tracers, weights, offsets, owner, codes):
        matrix = jnp.asarray(spread_matrix(tracers.shape[2]), BF16)
        body = jax.shard_map(
            on_device, mesh=mesh, in_specs=in_specs, out_specs=split, check_vma=False
        )
        return body(tracers, weights, offsets, owner, codes, matrix)

    return run
```

```python
import functools

import jax
import jax.numpy as jnp
import numpy as np
from jax import lax
from jax.experimental import pallas as pl
from jax.experimental.pallas import tpu as pltpu
from jax.sharding import PartitionSpec as P

HALO = 3
BLOCK_X = 4
BLOCK_Y = 16
PITCH = 24
LANES = 128
LEAD = 4
UNROLL = 4
BF16 = jnp.bfloat16
F32 = jnp.float32

STENCILS = [
    {(0, 0): 1.0},
    {(1, 0): 0.5, (-1, 0): -0.5},
    {(0, 1): 0.5, (0, -1): -0.5},
    {(1, 0): 0.5, (0, 0): -1.0, (-1, 0): 0.5},
    {(0, 1): 0.5, (0, 0): -1.0, (0, -1): 0.5},
    {(1, 1): 0.25, (1, -1): -0.25, (-1, 1): -0.25, (-1, -1): 0.25},
]


def spread_matrix(levels):
    terms = 24 * levels
    rows = 2 * terms + 8 * pl.cdiv(2 * levels, 8)
    matrix = np.zeros((rows, 2 * levels * LANES), np.float32)
    for level in range(levels):
        for piece in range(4):
            for moment, stencil in enumerate(STENCILS):
                for (east, north), value in stencil.items():
                    lane = (piece // 2 + 1 + east) * PITCH + piece % 2 + 1 + north
                    row = 24 * level + 6 * piece + moment
                    matrix[row, level * LANES + lane] += value
                    matrix[terms + row, level * LANES + lane] += value
        first = (levels + level) * LANES
        matrix[2 * terms + 2 * level, first : first + LANES] = PITCH
        matrix[2 * terms + 2 * level + 1, first : first + LANES] = 1
    return matrix


def load_kernel(count, ends, run, owner_ref, codes_ref, cells_ref, weights_ref, offsets_ref,
                matrix_ref, after_ref, table_ref, inner_ref, weights_out, offsets_out, matrix_out,
                owner, codes, sems):
    del after_ref
    index, place = lax.axis_index("gx"), lax.axis_index("gy")
    last = cells_ref.shape[0] - HALO
    pairs = [
        (owner_ref, owner),
        (codes_ref, codes),
        (cells_ref.at[pl.ds(jnp.where(index % 2 == 0, last, 0), HALO)], inner_ref),
        (weights_ref, weights_out),
        (offsets_ref, offsets_out),
        (matrix_ref, matrix_out),
    ]
    copies = [pltpu.make_async_copy(a, b, sems.at[at]) for at, (a, b) in enumerate(pairs)]
    for copy in copies:
        copy.start()
    copies[0].wait()
    copies[1].wait()
    side = jnp.where(place == 0, 0, 1)
    window = Window(cells_ref.shape[0], 0, count, run, None)
    target = lax.rem(index + count // 2, count)
    is_end = jnp.logical_or(place == 0, place == ends - 1)
    code = jnp.where(is_end, codes[side, index], 0)
    lines = [window.start(owner[side, target]), window.start(owner[side, index]), code]
    for at, line in enumerate(lines):
        table_ref[at : at + 1] = jnp.full((1, LANES), line, jnp.int32)
    for copy in copies[2:]:
        copy.wait()


def band_kernel(levels, rows, weights_ref, offsets_ref, matrix_ref, after_ref, band_ref):
    del after_ref
    groups = weights_ref.shape[0] // UNROLL
    y_blocks = rows // BLOCK_Y
    lane = lax.broadcasted_iota(jnp.int32, (rows, LANES), 1)
    row_in = lax.broadcasted_iota(jnp.int32, (rows, LANES), 0) % BLOCK_Y
    base = lane - row_in - 2 * PITCH - 2
    pad = matrix_ref.shape[0] - 2 * weights_ref.shape[1] - offsets_ref.shape[1]

    def column(x):
        weights = weights_ref[x]
        high = weights.astype(BF16).astype(F32)
        stacked = jnp.concatenate(
            [high, weights - high, offsets_ref[x].astype(F32), jnp.zeros((pad, rows), F32)], axis=0
        ).astype(BF16)
        spread = lax.dot_general(
            stacked, matrix_ref[...], (((0,), (0,)), ((), ())), preferred_element_type=F32
        )
        block, inner = x // BLOCK_X, x % BLOCK_X
        at = pl.multiple_of(inner * BLOCK_Y, BLOCK_Y)
        low = pl.multiple_of(at + BLOCK_X * BLOCK_Y, BLOCK_Y)
        for level in range(levels):
            points = spread[:, level * LANES : (level + 1) * LANES]
            first = (levels + level) * LANES
            shift = spread[:, first : first + LANES].astype(jnp.int32)
            for y in range(y_blocks):
                mine = slice(y * BLOCK_Y, (y + 1) * BLOCK_Y)
                index = base[mine] - shift[mine] - inner * PITCH
                picked = jnp.take_along_axis(
                    points[mine], index & (LANES - 1), axis=1, mode="promise_in_bounds"
                )
                top = picked.astype(BF16).astype(F32)
                rest = picked - top
                here = index >= 0
                slot = (block * y_blocks + y) * levels + level
                for part in range(2):
                    lanes = slice(part * LANES, (part + 1) * LANES)
                    keep = here if part == 0 else jnp.logical_not(here)
                    band_ref[slot, pl.ds(at, BLOCK_Y), lanes] = jnp.where(keep, top, 0.0).astype(BF16)
                    band_ref[slot, pl.ds(low, BLOCK_Y), lanes] = jnp.where(keep, rest, 0.0).astype(BF16)

    def group_of(group, carry):
        for step in range(UNROLL):
            column(group * UNROLL + step)
        return carry

    lax.fori_loop(0, groups, group_of, 0)


def pack_kernel(cells_ref, edges_ref, message_ref, outer_ref, low_ref, high_ref, sems):
    cols, rows, _ = cells_ref.shape
    width = edges_ref.shape[0] // cols // 2
    deep = low_ref.shape[1]
    even, low = lax.axis_index("gx") % 2 == 0, lax.axis_index("gy") == 0
    last = cols - HALO
    copies = [
        pltpu.make_async_copy(cells_ref.at[:, pl.ds(0, deep)], low_ref, sems.at[0]),
        pltpu.make_async_copy(cells_ref.at[:, pl.ds(rows - deep, deep)], high_ref, sems.at[1]),
        pltpu.make_async_copy(
            cells_ref.at[pl.ds(jnp.where(even, 0, last), HALO)], outer_ref, sems.at[2]
        ),
    ]
    for copy in copies:
        copy.start()
    for copy in copies[:2]:
        copy.wait()
    for col in range(cols):
        at = 2 * width * col
        bottom, top = low_ref[col, :width], high_ref[col, deep - width :]
        edges_ref[at : at + width] = bottom
        edges_ref[at + width : at + 2 * width] = top
        message_ref[width * col : width * (col + 1)] = jnp.where(low, bottom, top)
    at = width * cols
    for col in range(HALO):
        for ref in (low_ref.at[:, :width], high_ref.at[:, deep - width :]):
            edge = jnp.where(even, ref[col], ref[last + col])
            message_ref[at : at + width] = edge
            at += width
    clear(message_ref, at)
    copies[2].wait()


def clear(ref, at):
    if at < ref.shape[0]:
        ref[at:] = jnp.zeros((ref.shape[0] - at, LANES), F32)


def relay_kernel(cols, width, edges_ref, message_ref, got_ref, after_ref, relay_ref):
    del after_ref
    even = lax.axis_index("gx") % 2 == 0
    corner, strip = 2 * width * HALO, width * cols
    edges = 2 * strip
    relay_ref[:corner] = jnp.where(even, edges_ref[edges - corner : edges], edges_ref[:corner])
    relay_ref[corner : corner + strip] = message_ref[:strip]
    relay_ref[corner + strip : corner + 2 * strip] = got_ref[:strip]
    clear(relay_ref, corner + 2 * strip)


def join_kernel(cols, width, message_ref, got_ref, other_ref, run_ref):
    even = lax.axis_index("gx") % 2 == 0
    corner, strip = 2 * width * HALO, width * cols
    mine, far = message_ref[:strip], got_ref[:strip]
    near = other_ref[corner : corner + strip]
    beyond = other_ref[corner + strip : corner + 2 * strip]
    pairs = ((far, beyond), (mine, near), (near, mine), (beyond, far))
    for at, (a, b) in enumerate(pairs):
        run_ref[at * strip : (at + 1) * strip] = jnp.where(even, a, b)


class Window:
    def __init__(self, cols, width, count, run, held):
        self.cols, self.width, self.total, self.run = cols, width, count * cols, run
        self.held = held
        index = lax.axis_index("gx")
        self.first = index - index % 2 - 1

    def start(self, owner):
        return lax.rem((owner - self.first) * self.cols - HALO + 2 * self.total, self.total)

    def column(self, start, step):
        at = start + step
        at = jnp.where(at >= self.total, at - self.total, at)
        row = jnp.minimum(at, self.run * self.cols - 1) * self.width
        return at < self.run * self.cols, self.held[pl.ds(row, self.width)]


def rows_kernel(cols, width, count, ends, run, table_ref, edges_ref, other_ref, got_ref, run_ref,
                first_ref, second_ref):
    even, place = lax.axis_index("gx") % 2 == 0, lax.axis_index("gy")
    flat_place = place % 2 == 0
    strip = width * cols

    def rows(ref, at, top):
        return jnp.where(top, ref[at + width : at + 2 * width], ref[at : at + width])

    def column(u, top):
        if HALO <= u < HALO + cols:
            return rows(edges_ref, 2 * width * (u - HALO), top)
        col = u if u < HALO else u - HALO - cols
        near = rows(other_ref, 2 * width * col, top)
        far = rows(got_ref, strip + 2 * width * col, top)
        return jnp.where(even == (u < HALO), far, near)

    wide = cols + 2 * HALO
    window = Window(cols, width, count, run, run_ref)
    start = table_ref[0:1, 0:1][0, 0]
    is_end = jnp.logical_or(place == 0, place == ends - 1)
    for u in range(wide):
        to = slice(u * width, (u + 1) * width)
        first_ref[to] = column(u, flat_place)
        _, glued = window.column(start, u)
        second_ref[to] = jnp.where(is_end, glued, column(u, jnp.logical_not(flat_place)))
    clear(first_ref, wide * width)
    clear(second_ref, wide * width)


def block_sum(field_ref, band_ref, x, y, y_blocks, levels, level):
    size = BLOCK_X * BLOCK_Y
    reach = BLOCK_X + 2 * HALO
    begin = (y * BLOCK_Y + LEAD - HALO) * levels + level
    points = jnp.concatenate(
        [
            field_ref[x * BLOCK_X + c, pl.ds(begin, PITCH, stride=levels), :]
            for c in range(reach)
        ]
        + [jnp.zeros((2 * LANES - reach * PITCH, LANES), F32)],
        axis=0,
    )
    top = points.astype(BF16)
    rest = (points - top.astype(F32)).astype(BF16)
    band = band_ref[(x * y_blocks + y) * levels + level]
    product = jnp.dot(band, jnp.concatenate([top, rest], axis=1), preferred_element_type=F32)
    return product[:size, :LANES] + (product[:size, LANES:] + product[size:, :LANES])


def remap_rows(field_ref, band_ref, stage_ref, out_ref, sems, levels, y_blocks, which):
    x_blocks = stage_ref.shape[1] // BLOCK_X
    deep = BLOCK_Y * levels
    copies = []
    for at, y in enumerate(which):
        for level in range(levels):
            for x in range(x_blocks):
                total = block_sum(field_ref, band_ref, x, y, y_blocks, levels, level)
                for c in range(BLOCK_X):
                    stage_ref[at, x * BLOCK_X + c, pl.ds(level, BLOCK_Y, stride=levels), :] = total[
                        c * BLOCK_Y : (c + 1) * BLOCK_Y
                    ]
        copies.append(
            pltpu.make_async_copy(
                stage_ref.at[at], out_ref.at[:, pl.ds(y * deep, deep)], sems.at[at]
            )
        )
        copies[-1].start()
    for copy in copies:
        copy.wait()


def middle_kernel(levels, cells_ref, inner_ref, outer_ref, band_ref, after_ref, out_ref, field_ref,
                  stage_ref, sems):
    del after_ref
    cols, rows, _ = cells_ref.shape
    lead = LEAD * levels
    even = lax.axis_index("gx") % 2 == 0
    for col in range(cols):
        field_ref[HALO + col, lead : lead + rows] = cells_ref[col]
    for col in range(HALO):
        inner, outer = inner_ref[col], outer_ref[col]
        field_ref[col, lead : lead + rows] = jnp.where(even, outer, inner)
        field_ref[HALO + cols + col, lead : lead + rows] = jnp.where(even, inner, outer)
    y_blocks = rows // levels // BLOCK_Y
    remap_rows(
        field_ref, band_ref, stage_ref, out_ref, sems, levels, y_blocks, range(1, y_blocks - 1)
    )


def edge_kernel(levels, cols, rows, count, ends, run, table_ref, first_ref, second_ref, run_ref,
                band_ref, field_in, out_in, field_ref, out_ref, stage_ref, sems):
    del field_in, out_in
    width = HALO * levels
    lead = LEAD * levels
    place = lax.axis_index("gy")
    flat_place = place % 2 == 0
    wide = cols + 2 * HALO
    window = Window(cols, width, count, run, run_ref)
    start, code = table_ref[1:2, 0:1][0, 0], table_ref[2:3, 0:1][0, 0]
    is_end = jnp.logical_or(place == 0, place == ends - 1)
    mirrored = code % 2 == 1
    flipped = code // 2 % 2 == 1
    tail = field_ref.shape[1] - lead - rows - width
    for u in range(wide):
        plain = first_ref[u * width : (u + 1) * width]
        step = jnp.where(mirrored, wide - 1 - u, u)
        held, glued = window.column(start, step)
        come = second_ref[pl.ds(step * width, width)]
        strip = jnp.where(jnp.logical_and(is_end, held), glued, come)
        turned = jnp.concatenate(
            [strip[levels * r : levels * (r + 1)] for r in reversed(range(HALO))], axis=0
        )
        strip = jnp.where(flipped, turned, strip)
        field_ref[u, lead - width : lead] = jnp.where(flat_place, strip, plain)
        field_ref[u, lead + rows : lead + rows + width] = jnp.where(flat_place, plain, strip)
        field_ref[u, lead + rows + width :] = jnp.zeros((tail, LANES), F32)
    y_blocks = rows // levels // BLOCK_Y
    remap_rows(
        field_ref, band_ref, stage_ref, out_ref, sems, levels, y_blocks, (0, y_blocks - 1)
    )


def grant(mebibytes):
    return pltpu.CompilerParams(vmem_limit_bytes=mebibytes << 20)


def takes(microseconds):
    return pl.CostEstimate(
        flops=0, bytes_accessed=int(microseconds * 3_000_000), transcendentals=0
    )


def in_hbm(array):
    return pltpu.with_memory_space_constraint(array, pltpu.HBM)


VMEM = pl.BlockSpec(memory_space=pltpu.VMEM)
HBM = pl.BlockSpec(memory_space=pltpu.HBM)
ANY = pl.BlockSpec(memory_space=pl.ANY)
SMEM = pl.BlockSpec(memory_space=pltpu.SMEM)


def shaped(*shape, dtype=F32):
    return jax.ShapeDtypeStruct(shape, dtype)


def eights(rows):
    return 8 * pl.cdiv(rows, 8)


def on_device(tracers, weights, offsets, owner, codes, matrix):
    cols, rows, levels, lanes = tracers.shape
    width = HALO * levels
    count, ends = lax.axis_size("gx"), lax.axis_size("gy")
    axes = ("gx", "gy")
    cells = tracers.reshape(cols, rows * levels, lanes)
    partner = [(i, i ^ 1) for i in range(count)]
    across = [(i, (i + 1) % count if i % 2 else (i - 1) % count) for i in range(count)]
    first_swap = [(i * ends + j, i * ends + (j ^ 1)) for i in range(count) for j in range(ends)]
    second_swap = []
    for i in range(count):
        for j in range(ends):
            if j in (0, ends - 1):
                second_swap.append((i * ends + j, (i + count // 2) % count * ends + j))
            else:
                second_swap.append((i * ends + j, i * ends + (j + 1 if j % 2 else j - 1)))

    deep = eights(width)
    strip, corner = width * cols, 2 * width * HALO
    columns = shaped(HALO, rows * levels, lanes)
    edges, message, outer = pl.pallas_call(
        pack_kernel,
        out_shape=(shaped(2 * strip, lanes), shaped(eights(strip + corner), lanes), columns),
        in_specs=[HBM],
        out_specs=(VMEM, VMEM, VMEM),
        scratch_shapes=[
            pltpu.VMEM((cols, deep, lanes), F32),
            pltpu.VMEM((cols, deep, lanes), F32),
            pltpu.SemaphoreType.DMA((3,)),
        ],
        name="pack",
        compiler_params=grant(4),
        cost_estimate=takes(1.0),
    )(in_hbm(cells))
    got = lax.ppermute(message, "gx", across)
    outer_got = lax.ppermute(outer, "gx", across)

    run = 4
    held = max(run, count // 2)
    weights = jnp.swapaxes(weights, 1, 2)
    offsets = jnp.swapaxes(offsets, 1, 2)
    table, inner, weights, offsets, matrix = pl.pallas_call(
        functools.partial(load_kernel, count, ends, held),
        out_shape=(
            shaped(8, lanes, dtype=jnp.int32),
            columns,
            shaped(*weights.shape),
            shaped(*offsets.shape, dtype=jnp.int32),
            shaped(*matrix.shape, dtype=BF16),
        ),
        in_specs=[HBM] * 6 + [ANY],
        out_specs=(VMEM,) * 5,
        scratch_shapes=[
            pltpu.SMEM(owner.shape, jnp.int32),
            pltpu.SMEM(codes.shape, jnp.int32),
            pltpu.SemaphoreType.DMA((6,)),
        ],
        name="load",
        compiler_params=grant(4),
        cost_estimate=takes(1.0),
    )(*[in_hbm(a) for a in (owner, codes, cells, weights, offsets, matrix)], message)

    relay = pl.pallas_call(
        functools.partial(relay_kernel, cols, width),
        out_shape=shaped(eights(corner + 2 * strip), lanes),
        in_specs=[VMEM] * 3 + [ANY],
        out_specs=VMEM,
        name="relay",
        compiler_params=grant(2),
        cost_estimate=takes(0.5),
    )(edges, message, got, table)
    other = lax.ppermute(relay, "gx", partner)
    inner_got = lax.ppermute(inner, "gx", partner)

    ring = pl.pallas_call(
        functools.partial(join_kernel, cols, width),
        out_shape=shaped(run * strip, lanes),
        in_specs=[VMEM] * 3,
        out_specs=VMEM,
        name="join",
        compiler_params=grant(2),
        cost_estimate=takes(0.5),
    )(message, got, other)
    while run < held:
        shift = run
        more = lax.ppermute(ring, "gx", [((i + shift) % count, i) for i in range(count)])
        ring = jnp.concatenate([ring, more])
        run *= 2

    z_rows = eights(width * (cols + 2 * HALO))
    first, second = pl.pallas_call(
        functools.partial(rows_kernel, cols, width, count, ends, run),
        out_shape=(shaped(z_rows, lanes), shaped(z_rows, lanes)),
        in_specs=[VMEM] * 5,
        out_specs=(VMEM, VMEM),
        name="rows",
        cost_estimate=takes(1.0),
        compiler_params=grant(2 * pl.cdiv(run, 8)),
    )(table, edges, other, got, ring)
    first_got = lax.ppermute(first, axes, first_swap)
    second_got = lax.ppermute(second, axes, second_swap)

    y_blocks = rows // BLOCK_Y
    slots = cols // BLOCK_X * y_blocks * levels
    band = pl.pallas_call(
        functools.partial(band_kernel, levels, rows),
        out_shape=shaped(slots, 2 * BLOCK_X * BLOCK_Y, 2 * LANES, dtype=BF16),
        in_specs=[VMEM] * 3 + [ANY],
        out_specs=VMEM,
        name="band",
        compiler_params=grant(6),
        cost_estimate=takes(1.5),
    )(weights, offsets, matrix, first)

    field_rows = eights((LEAD + rows + HALO + PITCH - BLOCK_Y - 2 * HALO) * levels)
    field_shape = shaped(cols + 2 * HALO, field_rows, lanes)
    out_shape = shaped(cols, rows * levels, lanes)
    stage = (cols, BLOCK_Y * levels, lanes)
    partial, field = pl.pallas_call(
        functools.partial(middle_kernel, levels),
        out_shape=(out_shape, field_shape),
        in_specs=[VMEM] * 4 + [ANY],
        out_specs=(HBM, VMEM),
        scratch_shapes=[
            pltpu.VMEM((y_blocks - 2, *stage), F32),
            pltpu.SemaphoreType.DMA((y_blocks - 2,)),
        ],
        name="middle",
        cost_estimate=takes(2.0),
        compiler_params=grant(6),
    )(cells, inner_got, outer_got, band, first)
    _, updated = pl.pallas_call(
        functools.partial(edge_kernel, levels, cols, rows * levels, count, ends, run),
        out_shape=(field_shape, out_shape),
        in_specs=[VMEM] * 6 + [HBM],
        out_specs=(VMEM, HBM),
        scratch_shapes=[pltpu.VMEM((2, *stage), F32), pltpu.SemaphoreType.DMA((2,))],
        input_output_aliases={5: 0, 6: 1},
        name="edge",
        cost_estimate=takes(2.0),
        compiler_params=grant(6),
    )(table, first_got, second_got, ring, band, field, partial)
    return updated.reshape(cols, rows, levels, lanes)


def solution(mesh):
    split = P("gx", "gy", None, None)
    in_specs = (split, P("gx", "gy", None), P("gx", "gy", None), P(), P(), P())


    def run(tracers, weights, offsets, owner, codes):
        matrix = jnp.asarray(spread_matrix(tracers.shape[2]), BF16)
        body = jax.shard_map(
            on_device, mesh=mesh, in_specs=in_specs, out_specs=split, check_vma=False
        )
        return body(tracers, weights, offsets, owner, codes, matrix)

    return run
```

```python
import functools

import jax
import jax.numpy as jnp
import numpy as np
from jax import lax
from jax.experimental import pallas as pl
from jax.experimental.pallas import tpu as pltpu
from jax.sharding import PartitionSpec as P

HALO = 3
BLOCK_X = 4
BLOCK_Y = 16
PITCH = 24
LANES = 128
LEAD = 4
BF16 = jnp.bfloat16
F32 = jnp.float32

STENCILS = [
    {(0, 0): 1.0},
    {(1, 0): 0.5, (-1, 0): -0.5},
    {(0, 1): 0.5, (0, -1): -0.5},
    {(1, 0): 0.5, (0, 0): -1.0, (-1, 0): 0.5},
    {(0, 1): 0.5, (0, 0): -1.0, (0, -1): 0.5},
    {(1, 1): 0.25, (1, -1): -0.25, (-1, 1): -0.25, (-1, -1): 0.25},
]


def spread_matrix(levels):
    terms = 24 * levels
    rows = 2 * terms + 8 * pl.cdiv(2 * levels, 8)
    matrix = np.zeros((rows, 2 * levels * LANES), np.float32)
    for level in range(levels):
        for piece in range(4):
            for moment, stencil in enumerate(STENCILS):
                for (east, north), value in stencil.items():
                    lane = (piece // 2 + 1 + east) * PITCH + piece % 2 + 1 + north
                    row = 24 * level + 6 * piece + moment
                    matrix[row, level * LANES + lane] += value
                    matrix[terms + row, level * LANES + lane] += value
        first = (levels + level) * LANES
        matrix[2 * terms + 2 * level, first : first + LANES] = PITCH
        matrix[2 * terms + 2 * level + 1, first : first + LANES] = 1
    return matrix


def load_kernel(count, ends, run, owner_ref, codes_ref, cells_ref, weights_ref, offsets_ref,
                matrix_ref, after_ref, table_ref, inner_ref, weights_out, offsets_out, matrix_out,
                owner, codes, sems):
    del after_ref
    index, place = lax.axis_index("gx"), lax.axis_index("gy")
    last = cells_ref.shape[0] - HALO
    pairs = [
        (owner_ref, owner),
        (codes_ref, codes),
        (cells_ref.at[pl.ds(jnp.where(index % 2 == 0, last, 0), HALO)], inner_ref),
        (weights_ref, weights_out),
        (offsets_ref, offsets_out),
        (matrix_ref, matrix_out),
    ]
    copies = [pltpu.make_async_copy(a, b, sems.at[at]) for at, (a, b) in enumerate(pairs)]
    for copy in copies:
        copy.start()
    copies[0].wait()
    copies[1].wait()
    side = jnp.where(place == 0, 0, 1)
    window = Window(cells_ref.shape[0], 0, count, run, None)
    target = lax.rem(index + count // 2, count)
    is_end = jnp.logical_or(place == 0, place == ends - 1)
    code = jnp.where(is_end, codes[side, index], 0)
    lines = [window.start(owner[side, target]), window.start(owner[side, index]), code]
    for at, line in enumerate(lines):
        table_ref[at : at + 1] = jnp.full((1, LANES), line, jnp.int32)
    for copy in copies[2:]:
        copy.wait()


def band_kernel(levels, rows, block, weights_ref, offsets_ref, matrix_ref, after_ref, band_ref):
    del after_ref
    y_blocks = rows // BLOCK_Y
    lane = lax.broadcasted_iota(jnp.int32, (rows, LANES), 1)
    row_in = lax.broadcasted_iota(jnp.int32, (rows, LANES), 0) % BLOCK_Y
    base = lane - row_in - 2 * PITCH - 2
    pad = matrix_ref.shape[0] - 2 * weights_ref.shape[1] - offsets_ref.shape[1]

    def column(x):
        weights = weights_ref[x]
        high = weights.astype(BF16).astype(F32)
        stacked = jnp.concatenate(
            [high, weights - high, offsets_ref[x].astype(F32), jnp.zeros((pad, rows), F32)], axis=0
        ).astype(BF16)
        spread = lax.dot_general(
            stacked, matrix_ref[...], (((0,), (0,)), ((), ())), preferred_element_type=F32
        )
        inner = x % BLOCK_X
        at = inner * BLOCK_Y
        low = at + BLOCK_X * BLOCK_Y
        for level in range(levels):
            points = spread[:, level * LANES : (level + 1) * LANES]
            first = (levels + level) * LANES
            shift = spread[:, first : first + LANES].astype(jnp.int32)
            for y in range(y_blocks):
                mine = slice(y * BLOCK_Y, (y + 1) * BLOCK_Y)
                index = base[mine] - shift[mine] - inner * PITCH
                picked = jnp.take_along_axis(
                    points[mine], index & (LANES - 1), axis=1, mode="promise_in_bounds"
                )
                top = picked.astype(BF16).astype(F32)
                rest = picked - top
                here = index >= 0
                slot = y * levels + level
                for part in range(2):
                    lanes = slice(part * LANES, (part + 1) * LANES)
                    keep = here if part == 0 else jnp.logical_not(here)
                    band_ref[slot, at : at + BLOCK_Y, lanes] = jnp.where(keep, top, 0.0).astype(BF16)
                    band_ref[slot, low : low + BLOCK_Y, lanes] = jnp.where(keep, rest, 0.0).astype(BF16)

    for step in range(BLOCK_X):
        column(block * BLOCK_X + step)


def pack_kernel(cells_ref, edges_ref, message_ref, outer_ref, low_ref, high_ref, sems):
    cols, rows, _ = cells_ref.shape
    width = edges_ref.shape[0] // cols // 2
    deep = low_ref.shape[1]
    even, low = lax.axis_index("gx") % 2 == 0, lax.axis_index("gy") == 0
    last = cols - HALO
    copies = [
        pltpu.make_async_copy(cells_ref.at[:, pl.ds(0, deep)], low_ref, sems.at[0]),
        pltpu.make_async_copy(cells_ref.at[:, pl.ds(rows - deep, deep)], high_ref, sems.at[1]),
        pltpu.make_async_copy(
            cells_ref.at[pl.ds(jnp.where(even, 0, last), HALO)], outer_ref, sems.at[2]
        ),
    ]
    for copy in copies:
        copy.start()
    for copy in copies[:2]:
        copy.wait()
    for col in range(cols):
        at = 2 * width * col
        bottom, top = low_ref[col, :width], high_ref[col, deep - width :]
        edges_ref[at : at + width] = bottom
        edges_ref[at + width : at + 2 * width] = top
        message_ref[width * col : width * (col + 1)] = jnp.where(low, bottom, top)
    at = width * cols
    for col in range(HALO):
        for ref in (low_ref.at[:, :width], high_ref.at[:, deep - width :]):
            edge = jnp.where(even, ref[col], ref[last + col])
            message_ref[at : at + width] = edge
            at += width
    clear(message_ref, at)
    copies[2].wait()


def clear(ref, at):
    if at < ref.shape[0]:
        ref[at:] = jnp.zeros((ref.shape[0] - at, LANES), F32)


def relay_kernel(cols, width, edges_ref, message_ref, got_ref, after_ref, relay_ref):
    del after_ref
    even = lax.axis_index("gx") % 2 == 0
    corner, strip = 2 * width * HALO, width * cols
    edges = 2 * strip
    relay_ref[:corner] = jnp.where(even, edges_ref[edges - corner : edges], edges_ref[:corner])
    relay_ref[corner : corner + strip] = message_ref[:strip]
    relay_ref[corner + strip : corner + 2 * strip] = got_ref[:strip]
    clear(relay_ref, corner + 2 * strip)


def join_kernel(cols, width, message_ref, got_ref, other_ref, after_ref, run_ref):
    del after_ref
    even = lax.axis_index("gx") % 2 == 0
    corner, strip = 2 * width * HALO, width * cols
    mine, far = message_ref[:strip], got_ref[:strip]
    near = other_ref[corner : corner + strip]
    beyond = other_ref[corner + strip : corner + 2 * strip]
    pairs = ((far, beyond), (mine, near), (near, mine), (beyond, far))
    for at, (a, b) in enumerate(pairs):
        run_ref[at * strip : (at + 1) * strip] = jnp.where(even, a, b)


class Window:
    def __init__(self, cols, width, count, run, held):
        self.cols, self.width, self.total, self.run = cols, width, count * cols, run
        self.held = held
        index = lax.axis_index("gx")
        self.first = index - index % 2 - 1

    def start(self, owner):
        return lax.rem((owner - self.first) * self.cols - HALO + 2 * self.total, self.total)

    def column(self, start, step):
        at = start + step
        at = jnp.where(at >= self.total, at - self.total, at)
        row = jnp.minimum(at, self.run * self.cols - 1) * self.width
        return at < self.run * self.cols, self.held[pl.ds(row, self.width)]


def rows_kernel(cols, width, count, ends, run, table_ref, edges_ref, other_ref, got_ref, run_ref,
                first_ref, second_ref):
    even, place = lax.axis_index("gx") % 2 == 0, lax.axis_index("gy")
    flat_place = place % 2 == 0
    strip = width * cols

    def rows(ref, at, top):
        return jnp.where(top, ref[at + width : at + 2 * width], ref[at : at + width])

    def column(u, top):
        if HALO <= u < HALO + cols:
            return rows(edges_ref, 2 * width * (u - HALO), top)
        col = u if u < HALO else u - HALO - cols
        near = rows(other_ref, 2 * width * col, top)
        far = rows(got_ref, strip + 2 * width * col, top)
        return jnp.where(even == (u < HALO), far, near)

    wide = cols + 2 * HALO
    window = Window(cols, width, count, run, run_ref)
    start = table_ref[0:1, 0:1][0, 0]
    is_end = jnp.logical_or(place == 0, place == ends - 1)
    for u in range(wide):
        to = slice(u * width, (u + 1) * width)
        first_ref[to] = column(u, flat_place)
        _, glued = window.column(start, u)
        second_ref[to] = jnp.where(is_end, glued, column(u, jnp.logical_not(flat_place)))
    clear(first_ref, wide * width)
    clear(second_ref, wide * width)


def block_sum(field_ref, bands, x, y, levels, level):
    size = BLOCK_X * BLOCK_Y
    reach = BLOCK_X + 2 * HALO
    begin = (y * BLOCK_Y + LEAD - HALO) * levels + level
    points = jnp.concatenate(
        [
            field_ref[x * BLOCK_X + c, pl.ds(begin, PITCH, stride=levels), :]
            for c in range(reach)
        ]
        + [jnp.zeros((2 * LANES - reach * PITCH, LANES), F32)],
        axis=0,
    )
    top = points.astype(BF16)
    rest = (points - top.astype(F32)).astype(BF16)
    band = bands[x][y * levels + level]
    product = jnp.dot(band, jnp.concatenate([top, rest], axis=1), preferred_element_type=F32)
    return product[:size, :LANES] + (product[:size, LANES:] + product[size:, :LANES])


def remap_rows(field_ref, bands, stage_ref, out_ref, sems, levels, which):
    x_blocks = stage_ref.shape[1] // BLOCK_X
    deep = BLOCK_Y * levels
    copies = []
    for at, y in enumerate(which):
        for level in range(levels):
            for x in range(x_blocks):
                total = block_sum(field_ref, bands, x, y, levels, level)
                for c in range(BLOCK_X):
                    stage_ref[at, x * BLOCK_X + c, pl.ds(level, BLOCK_Y, stride=levels), :] = total[
                        c * BLOCK_Y : (c + 1) * BLOCK_Y
                    ]
        copies.append(
            pltpu.make_async_copy(
                stage_ref.at[at], out_ref.at[:, pl.ds(y * deep, deep)], sems.at[at]
            )
        )
        copies[-1].start()
    for copy in copies:
        copy.wait()


def middle_kernel(levels, cells_ref, inner_ref, outer_ref, after_ref, *refs):
    del after_ref
    *bands, out_ref, field_ref, stage_ref, sems = refs
    cols, rows, _ = cells_ref.shape
    lead = LEAD * levels
    even = lax.axis_index("gx") % 2 == 0
    for col in range(cols):
        field_ref[HALO + col, lead : lead + rows] = cells_ref[col]
    for col in range(HALO):
        inner, outer = inner_ref[col], outer_ref[col]
        field_ref[col, lead : lead + rows] = jnp.where(even, outer, inner)
        field_ref[HALO + cols + col, lead : lead + rows] = jnp.where(even, inner, outer)
    y_blocks = rows // levels // BLOCK_Y
    remap_rows(field_ref, bands, stage_ref, out_ref, sems, levels, range(1, y_blocks - 1))


def edge_kernel(levels, cols, rows, count, ends, run, table_ref, first_ref, second_ref, run_ref,
                field_in, out_in, *refs):
    del field_in, out_in
    *bands, field_ref, out_ref, stage_ref, sems = refs
    width = HALO * levels
    lead = LEAD * levels
    place = lax.axis_index("gy")
    flat_place = place % 2 == 0
    wide = cols + 2 * HALO
    window = Window(cols, width, count, run, run_ref)
    start, code = table_ref[1:2, 0:1][0, 0], table_ref[2:3, 0:1][0, 0]
    is_end = jnp.logical_or(place == 0, place == ends - 1)
    mirrored = code % 2 == 1
    flipped = code // 2 % 2 == 1
    tail = field_ref.shape[1] - lead - rows - width
    for u in range(wide):
        plain = first_ref[u * width : (u + 1) * width]
        step = jnp.where(mirrored, wide - 1 - u, u)
        held, glued = window.column(start, step)
        come = second_ref[pl.ds(step * width, width)]
        strip = jnp.where(jnp.logical_and(is_end, held), glued, come)
        turned = jnp.concatenate(
            [strip[levels * r : levels * (r + 1)] for r in reversed(range(HALO))], axis=0
        )
        strip = jnp.where(flipped, turned, strip)
        field_ref[u, lead - width : lead] = jnp.where(flat_place, strip, plain)
        field_ref[u, lead + rows : lead + rows + width] = jnp.where(flat_place, plain, strip)
        field_ref[u, lead + rows + width :] = jnp.zeros((tail, LANES), F32)
    y_blocks = rows // levels // BLOCK_Y
    remap_rows(field_ref, bands, stage_ref, out_ref, sems, levels, (0, y_blocks - 1))


def grant(mebibytes):
    return pltpu.CompilerParams(vmem_limit_bytes=mebibytes << 20)


def takes(microseconds):
    return pl.CostEstimate(
        flops=0, bytes_accessed=int(microseconds * 3_000_000), transcendentals=0
    )


def in_hbm(array):
    return pltpu.with_memory_space_constraint(array, pltpu.HBM)


VMEM = pl.BlockSpec(memory_space=pltpu.VMEM)
HBM = pl.BlockSpec(memory_space=pltpu.HBM)
ANY = pl.BlockSpec(memory_space=pl.ANY)
SMEM = pl.BlockSpec(memory_space=pltpu.SMEM)


def shaped(*shape, dtype=F32):
    return jax.ShapeDtypeStruct(shape, dtype)


def eights(rows):
    return 8 * pl.cdiv(rows, 8)


def on_device(tracers, weights, offsets, owner, codes, matrix):
    cols, rows, levels, lanes = tracers.shape
    width = HALO * levels
    count, ends = lax.axis_size("gx"), lax.axis_size("gy")
    axes = ("gx", "gy")
    cells = tracers.reshape(cols, rows * levels, lanes)
    partner = [(i, i ^ 1) for i in range(count)]
    across = [(i, (i + 1) % count if i % 2 else (i - 1) % count) for i in range(count)]
    first_swap = [(i * ends + j, i * ends + (j ^ 1)) for i in range(count) for j in range(ends)]
    second_swap = []
    for i in range(count):
        for j in range(ends):
            if j in (0, ends - 1):
                second_swap.append((i * ends + j, (i + count // 2) % count * ends + j))
            else:
                second_swap.append((i * ends + j, i * ends + (j + 1 if j % 2 else j - 1)))

    deep = eights(width)
    strip, corner = width * cols, 2 * width * HALO
    columns = shaped(HALO, rows * levels, lanes)
    edges, message, outer = pl.pallas_call(
        pack_kernel,
        out_shape=(shaped(2 * strip, lanes), shaped(eights(strip + corner), lanes), columns),
        in_specs=[HBM],
        out_specs=(VMEM, VMEM, VMEM),
        scratch_shapes=[
            pltpu.VMEM((cols, deep, lanes), F32),
            pltpu.VMEM((cols, deep, lanes), F32),
            pltpu.SemaphoreType.DMA((3,)),
        ],
        name="pack",
        compiler_params=grant(4),
        cost_estimate=takes(1.0),
    )(in_hbm(cells))
    got = lax.ppermute(message, "gx", across)
    outer_got = lax.ppermute(outer, "gx", across)

    run = 4
    held = max(run, count // 2)
    weights = jnp.swapaxes(weights, 1, 2)
    offsets = jnp.swapaxes(offsets, 1, 2)
    table, inner, weights, offsets, matrix = pl.pallas_call(
        functools.partial(load_kernel, count, ends, held),
        out_shape=(
            shaped(8, lanes, dtype=jnp.int32),
            columns,
            shaped(*weights.shape),
            shaped(*offsets.shape, dtype=jnp.int32),
            shaped(*matrix.shape, dtype=BF16),
        ),
        in_specs=[HBM] * 6 + [ANY],
        out_specs=(VMEM,) * 5,
        scratch_shapes=[
            pltpu.SMEM(owner.shape, jnp.int32),
            pltpu.SMEM(codes.shape, jnp.int32),
            pltpu.SemaphoreType.DMA((6,)),
        ],
        name="load",
        compiler_params=grant(4),
        cost_estimate=takes(1.0),
    )(*[in_hbm(a) for a in (owner, codes, cells, weights, offsets, matrix)], message)

    x_blocks, y_blocks = cols // BLOCK_X, rows // BLOCK_Y

    def band_of(block, after):
        return pl.pallas_call(
            functools.partial(band_kernel, levels, rows, block),
            out_shape=shaped(y_blocks * levels, 2 * BLOCK_X * BLOCK_Y, 2 * LANES, dtype=BF16),
            in_specs=[VMEM] * 3 + [ANY],
            out_specs=VMEM,
            name="band",
            compiler_params=grant(4),
            cost_estimate=takes(0.5),
        )(weights, offsets, matrix, after)

    bands = [band_of(0, table)]
    relay = pl.pallas_call(
        functools.partial(relay_kernel, cols, width),
        out_shape=shaped(eights(corner + 2 * strip), lanes),
        in_specs=[VMEM] * 3 + [ANY],
        out_specs=VMEM,
        name="relay",
        compiler_params=grant(2),
        cost_estimate=takes(0.5),
    )(edges, message, got, bands[0])
    other = lax.ppermute(relay, "gx", partner)
    inner_got = lax.ppermute(inner, "gx", partner)

    bands.append(band_of(1, relay))
    ring = pl.pallas_call(
        functools.partial(join_kernel, cols, width),
        out_shape=shaped(run * strip, lanes),
        in_specs=[VMEM] * 3 + [ANY],
        out_specs=VMEM,
        name="join",
        compiler_params=grant(2),
        cost_estimate=takes(0.5),
    )(message, got, other, bands[1])
    while run < held:
        shift = run
        more = lax.ppermute(ring, "gx", [((i + shift) % count, i) for i in range(count)])
        ring = jnp.concatenate([ring, more])
        run *= 2

    z_rows = eights(width * (cols + 2 * HALO))
    first, second = pl.pallas_call(
        functools.partial(rows_kernel, cols, width, count, ends, run),
        out_shape=(shaped(z_rows, lanes), shaped(z_rows, lanes)),
        in_specs=[VMEM] * 5,
        out_specs=(VMEM, VMEM),
        name="rows",
        cost_estimate=takes(1.0),
        compiler_params=grant(2 * pl.cdiv(run, 8)),
    )(table, edges, other, got, ring)
    first_got = lax.ppermute(first, axes, first_swap)
    second_got = lax.ppermute(second, axes, second_swap)

    bands.extend(band_of(block, second) for block in range(2, x_blocks))

    field_rows = eights((LEAD + rows + HALO + PITCH - BLOCK_Y - 2 * HALO) * levels)
    field_shape = shaped(cols + 2 * HALO, field_rows, lanes)
    out_shape = shaped(cols, rows * levels, lanes)
    stage = (cols, BLOCK_Y * levels, lanes)
    partial, field = pl.pallas_call(
        functools.partial(middle_kernel, levels),
        out_shape=(out_shape, field_shape),
        in_specs=[VMEM] * 3 + [ANY] + [VMEM] * x_blocks,
        out_specs=(HBM, VMEM),
        scratch_shapes=[
            pltpu.VMEM((y_blocks - 2, *stage), F32),
            pltpu.SemaphoreType.DMA((y_blocks - 2,)),
        ],
        name="middle",
        cost_estimate=takes(2.0),
        compiler_params=grant(6),
    )(cells, inner_got, outer_got, second, *bands)
    _, updated = pl.pallas_call(
        functools.partial(edge_kernel, levels, cols, rows * levels, count, ends, run),
        out_shape=(field_shape, out_shape),
        in_specs=[VMEM] * 5 + [HBM] + [VMEM] * x_blocks,
        out_specs=(VMEM, HBM),
        scratch_shapes=[pltpu.VMEM((2, *stage), F32), pltpu.SemaphoreType.DMA((2,))],
        input_output_aliases={4: 0, 5: 1},
        name="edge",
        cost_estimate=takes(2.0),
        compiler_params=grant(6),
    )(table, first_got, second_got, ring, field, partial, *bands)
    return updated.reshape(cols, rows, levels, lanes)


def solution(mesh):
    split = P("gx", "gy", None, None)
    in_specs = (split, P("gx", "gy", None), P("gx", "gy", None), P(), P(), P())


    def run(tracers, weights, offsets, owner, codes):
        matrix = jnp.asarray(spread_matrix(tracers.shape[2]), BF16)
        body = jax.shard_map(
            on_device, mesh=mesh, in_specs=in_specs, out_specs=split, check_vma=False
        )
        return body(tracers, weights, offsets, owner, codes, matrix)

    return run
```

```python
import functools

import jax
import jax.numpy as jnp
import numpy as np
from jax import lax
from jax.experimental import pallas as pl
from jax.experimental.pallas import tpu as pltpu
from jax.sharding import PartitionSpec as P

HALO = 3
BLOCK_X = 4
BLOCK_Y = 16
PITCH = 24
LANES = 128
LEAD = 4
BF16 = jnp.bfloat16
F32 = jnp.float32

STENCILS = [
    {(0, 0): 1.0},
    {(1, 0): 0.5, (-1, 0): -0.5},
    {(0, 1): 0.5, (0, -1): -0.5},
    {(1, 0): 0.5, (0, 0): -1.0, (-1, 0): 0.5},
    {(0, 1): 0.5, (0, 0): -1.0, (0, -1): 0.5},
    {(1, 1): 0.25, (1, -1): -0.25, (-1, 1): -0.25, (-1, -1): 0.25},
]


def spread_matrix(levels):
    terms = 24 * levels
    rows = 2 * terms + 8 * pl.cdiv(2 * levels, 8)
    matrix = np.zeros((rows, 2 * levels * LANES), np.float32)
    for level in range(levels):
        for piece in range(4):
            for moment, stencil in enumerate(STENCILS):
                for (east, north), value in stencil.items():
                    lane = (piece // 2 + 1 + east) * PITCH + piece % 2 + 1 + north
                    row = 24 * level + 6 * piece + moment
                    matrix[row, level * LANES + lane] += value
                    matrix[terms + row, level * LANES + lane] += value
        first = (levels + level) * LANES
        matrix[2 * terms + 2 * level, first : first + LANES] = PITCH
        matrix[2 * terms + 2 * level + 1, first : first + LANES] = 1
    return matrix


def load_kernel(count, ends, run, owner_ref, codes_ref, cells_ref, weights_ref, offsets_ref,
                matrix_ref, after_ref, table_ref, inner_ref, weights_out, offsets_out, matrix_out,
                field_ref, owner, codes, sems):
    del after_ref
    index, place = lax.axis_index("gx"), lax.axis_index("gy")
    cols, rows, _ = cells_ref.shape
    lead = LEAD * (weights_ref.shape[1] // 24)
    last = cols - HALO
    pairs = [
        (owner_ref, owner),
        (codes_ref, codes),
        (cells_ref.at[pl.ds(jnp.where(index % 2 == 0, last, 0), HALO)], inner_ref),
        (weights_ref, weights_out),
        (offsets_ref, offsets_out),
        (matrix_ref, matrix_out),
    ]
    for col in range(0, cols, BLOCK_X):
        to = field_ref.at[pl.ds(HALO + col, BLOCK_X), pl.ds(lead, rows)]
        pairs.append((cells_ref.at[pl.ds(col, BLOCK_X)], to))
    copies = [pltpu.make_async_copy(a, b, sems.at[at]) for at, (a, b) in enumerate(pairs)]
    for copy in copies:
        copy.start()
    copies[0].wait()
    copies[1].wait()
    side = jnp.where(place == 0, 0, 1)
    window = Window(cells_ref.shape[0], 0, count, run, None)
    target = lax.rem(index + count // 2, count)
    is_end = jnp.logical_or(place == 0, place == ends - 1)
    code = jnp.where(is_end, codes[side, index], 0)
    lines = [window.start(owner[side, target]), window.start(owner[side, index]), code]
    for at, line in enumerate(lines):
        table_ref[at : at + 1] = jnp.full((1, LANES), line, jnp.int32)
    for copy in copies[2:]:
        copy.wait()


def band_kernel(levels, rows, block, weights_ref, offsets_ref, matrix_ref, after_ref, band_ref):
    del after_ref
    y_blocks = rows // BLOCK_Y
    lane = lax.broadcasted_iota(jnp.int32, (rows, LANES), 1)
    row_in = lax.broadcasted_iota(jnp.int32, (rows, LANES), 0) % BLOCK_Y
    base = lane - row_in - 2 * PITCH - 2
    pad = matrix_ref.shape[0] - 2 * weights_ref.shape[1] - offsets_ref.shape[1]

    def column(x):
        weights = weights_ref[x]
        high = weights.astype(BF16).astype(F32)
        stacked = jnp.concatenate(
            [high, weights - high, offsets_ref[x].astype(F32), jnp.zeros((pad, rows), F32)], axis=0
        ).astype(BF16)
        spread = lax.dot_general(
            stacked, matrix_ref[...], (((0,), (0,)), ((), ())), preferred_element_type=F32
        )
        inner = x % BLOCK_X
        at = inner * BLOCK_Y
        low = at + BLOCK_X * BLOCK_Y
        for level in range(levels):
            points = spread[:, level * LANES : (level + 1) * LANES]
            first = (levels + level) * LANES
            shift = spread[:, first : first + LANES].astype(jnp.int32)
            for y in range(y_blocks):
                mine = slice(y * BLOCK_Y, (y + 1) * BLOCK_Y)
                index = base[mine] - shift[mine] - inner * PITCH
                picked = jnp.take_along_axis(
                    points[mine], index & (LANES - 1), axis=1, mode="promise_in_bounds"
                )
                top = picked.astype(BF16).astype(F32)
                rest = picked - top
                here = index >= 0
                slot = y * levels + level
                for part in range(2):
                    lanes = slice(part * LANES, (part + 1) * LANES)
                    keep = here if part == 0 else jnp.logical_not(here)
                    band_ref[slot, at : at + BLOCK_Y, lanes] = jnp.where(keep, top, 0.0).astype(BF16)
                    band_ref[slot, low : low + BLOCK_Y, lanes] = jnp.where(keep, rest, 0.0).astype(BF16)

    for step in range(BLOCK_X):
        column(block * BLOCK_X + step)


def pack_kernel(cells_ref, edges_ref, message_ref, outer_ref, low_ref, high_ref, sems):
    cols, rows, _ = cells_ref.shape
    width = edges_ref.shape[0] // cols // 2
    deep = low_ref.shape[1]
    even, low = lax.axis_index("gx") % 2 == 0, lax.axis_index("gy") == 0
    last = cols - HALO
    copies = [
        pltpu.make_async_copy(cells_ref.at[:, pl.ds(0, deep)], low_ref, sems.at[0]),
        pltpu.make_async_copy(cells_ref.at[:, pl.ds(rows - deep, deep)], high_ref, sems.at[1]),
        pltpu.make_async_copy(
            cells_ref.at[pl.ds(jnp.where(even, 0, last), HALO)], outer_ref, sems.at[2]
        ),
    ]
    for copy in copies:
        copy.start()
    for copy in copies[:2]:
        copy.wait()
    for col in range(cols):
        at = 2 * width * col
        bottom, top = low_ref[col, :width], high_ref[col, deep - width :]
        edges_ref[at : at + width] = bottom
        edges_ref[at + width : at + 2 * width] = top
        message_ref[width * col : width * (col + 1)] = jnp.where(low, bottom, top)
    at = width * cols
    for col in range(HALO):
        for ref in (low_ref.at[:, :width], high_ref.at[:, deep - width :]):
            edge = jnp.where(even, ref[col], ref[last + col])
            message_ref[at : at + width] = edge
            at += width
    clear(message_ref, at)
    copies[2].wait()


def clear(ref, at):
    if at < ref.shape[0]:
        ref[at:] = jnp.zeros((ref.shape[0] - at, LANES), F32)


def relay_kernel(cols, width, edges_ref, message_ref, got_ref, after_ref, relay_ref, first_ref):
    del after_ref
    even = lax.axis_index("gx") % 2 == 0
    up = lax.axis_index("gy") % 2 == 0
    corner, strip = 2 * width * HALO, width * cols
    edges = 2 * strip
    relay_ref[:corner] = jnp.where(even, edges_ref[edges - corner : edges], edges_ref[:corner])
    relay_ref[corner : corner + strip] = message_ref[:strip]
    relay_ref[corner + strip : corner + 2 * strip] = got_ref[:strip]
    clear(relay_ref, corner + 2 * strip)
    for u in range(HALO + cols):
        ref, at = (got_ref, strip) if u < HALO else (edges_ref, -corner)
        at += 2 * width * u
        first_ref[u * width : (u + 1) * width] = jnp.where(
            up, ref[at + width : at + 2 * width], ref[at : at + width]
        )
    clear(first_ref, (HALO + cols) * width)


def turn_kernel(cols, width, first_ref, *refs):
    corner_ref = refs[-1]
    even = lax.axis_index("gx") % 2 == 0
    size = HALO * width
    last = (HALO + cols) * width
    corner_ref[:size] = jnp.where(even, first_ref[last - size : last], first_ref[size : 2 * size])
    clear(corner_ref, size)


def join_kernel(cols, width, message_ref, got_ref, other_ref, after_ref, run_ref):
    del after_ref
    even = lax.axis_index("gx") % 2 == 0
    corner, strip = 2 * width * HALO, width * cols
    mine, far = message_ref[:strip], got_ref[:strip]
    near = other_ref[corner : corner + strip]
    beyond = other_ref[corner + strip : corner + 2 * strip]
    pairs = ((far, beyond), (mine, near), (near, mine), (beyond, far))
    for at, (a, b) in enumerate(pairs):
        run_ref[at * strip : (at + 1) * strip] = jnp.where(even, a, b)


class Window:
    def __init__(self, cols, width, count, run, held):
        self.cols, self.width, self.total, self.run = cols, width, count * cols, run
        self.held = held
        index = lax.axis_index("gx")
        self.first = index - index % 2 - 1

    def start(self, owner):
        return lax.rem((owner - self.first) * self.cols - HALO + 2 * self.total, self.total)

    def column(self, start, step):
        at = start + step
        at = jnp.where(at >= self.total, at - self.total, at)
        row = jnp.minimum(at, self.run * self.cols - 1) * self.width
        return at < self.run * self.cols, self.held[pl.ds(row, self.width)]


def rows_kernel(cols, width, count, ends, run, table_ref, edges_ref, other_ref, got_ref, run_ref,
                second_ref):
    even, place = lax.axis_index("gx") % 2 == 0, lax.axis_index("gy")
    top = place % 2 == 1
    strip = width * cols

    def rows(ref, at, top):
        return jnp.where(top, ref[at + width : at + 2 * width], ref[at : at + width])

    def column(u, top):
        if HALO <= u < HALO + cols:
            return rows(edges_ref, 2 * width * (u - HALO), top)
        col = u if u < HALO else u - HALO - cols
        near = rows(other_ref, 2 * width * col, top)
        far = rows(got_ref, strip + 2 * width * col, top)
        return jnp.where(even == (u < HALO), far, near)

    wide = cols + 2 * HALO
    window = Window(cols, width, count, run, run_ref)
    start = table_ref[0:1, 0:1][0, 0]
    is_end = jnp.logical_or(place == 0, place == ends - 1)
    for u in range(wide):
        to = slice(u * width, (u + 1) * width)
        _, glued = window.column(start, u)
        second_ref[to] = jnp.where(is_end, glued, column(u, top))
    clear(second_ref, wide * width)


def block_sum(field_ref, bands, x, y, levels, level):
    size = BLOCK_X * BLOCK_Y
    reach = BLOCK_X + 2 * HALO
    begin = (y * BLOCK_Y + LEAD - HALO) * levels + level
    points = jnp.concatenate(
        [
            field_ref[x * BLOCK_X + c, pl.ds(begin, PITCH, stride=levels), :]
            for c in range(reach)
        ]
        + [jnp.zeros((2 * LANES - reach * PITCH, LANES), F32)],
        axis=0,
    )
    top = points.astype(BF16)
    rest = (points - top.astype(F32)).astype(BF16)
    band = bands[x][y * levels + level]
    product = jnp.dot(band, jnp.concatenate([top, rest], axis=1), preferred_element_type=F32)
    return product[:size, :LANES] + (product[:size, LANES:] + product[size:, :LANES])


def remap_blocks(field_ref, bands, stage_ref, levels, blocks, ready=None):
    for at, (x, y) in enumerate(blocks):
        for level in range(levels):
            total = block_sum(field_ref, bands, x, y, levels, level)
            for c in range(BLOCK_X):
                stage_ref[at, c, pl.ds(level, BLOCK_Y, stride=levels), :] = total[
                    c * BLOCK_Y : (c + 1) * BLOCK_Y
                ]
        if ready is not None:
            ready(at, x, y)


def middle_kernel(levels, blocks, inner_ref, outer_ref, after_ref, field_in, *refs):
    del after_ref, field_in
    *bands, field_ref, stage_ref = refs
    rows, wide = inner_ref.shape[1], field_ref.shape[0]
    lead = LEAD * levels
    even = lax.axis_index("gx") % 2 == 0
    for col in range(HALO):
        inner, outer = inner_ref[col], outer_ref[col]
        field_ref[col, lead : lead + rows] = jnp.where(even, outer, inner)
        field_ref[wide - HALO + col, lead : lead + rows] = jnp.where(even, inner, outer)
    remap_blocks(field_ref, bands, stage_ref, levels, blocks)


def edge_kernel(levels, cols, rows, count, ends, run, blocks, done, table_ref, first_ref, corner_ref,
                second_ref, run_ref, done_ref, field_in, *refs):
    del field_in
    *bands, field_ref, out_ref, stage_ref, sems = refs
    deep = BLOCK_Y * levels
    copies = []

    def put(source, x, y):
        to = out_ref.at[pl.ds(x * BLOCK_X, BLOCK_X), pl.ds(y * deep, deep)]
        copies.append(pltpu.make_async_copy(source, to, sems.at[len(copies)]))
        copies[-1].start()

    for at, (x, y) in enumerate(done):
        put(done_ref.at[at], x, y)
    width = HALO * levels
    lead = LEAD * levels
    even, place = lax.axis_index("gx") % 2 == 0, lax.axis_index("gy")
    flat_place = place % 2 == 0
    wide = cols + 2 * HALO
    window = Window(cols, width, count, run, run_ref)
    start, code = table_ref[1:2, 0:1][0, 0], table_ref[2:3, 0:1][0, 0]
    is_end = jnp.logical_or(place == 0, place == ends - 1)
    mirrored = code % 2 == 1
    flipped = code // 2 % 2 == 1
    tail = field_ref.shape[1] - lead - rows - width
    for u in range(wide):
        if HALO <= u < HALO + cols:
            plain = first_ref[u * width : (u + 1) * width]
        else:
            col = u if u < HALO else u - HALO - cols
            far = first_ref[col * width : (col + 1) * width]
            near = corner_ref[col * width : (col + 1) * width]
            plain = jnp.where(even == (u < HALO), far, near)
        step = jnp.where(mirrored, wide - 1 - u, u)
        held, glued = window.column(start, step)
        come = second_ref[pl.ds(step * width, width)]
        strip = jnp.where(jnp.logical_and(is_end, held), glued, come)
        turned = jnp.concatenate(
            [strip[levels * r : levels * (r + 1)] for r in reversed(range(HALO))], axis=0
        )
        strip = jnp.where(flipped, turned, strip)
        field_ref[u, lead - width : lead] = jnp.where(flat_place, strip, plain)
        field_ref[u, lead + rows : lead + rows + width] = jnp.where(flat_place, plain, strip)
        field_ref[u, lead + rows + width :] = jnp.zeros((tail, LANES), F32)
    remap_blocks(
        field_ref, bands, stage_ref, levels, blocks,
        lambda at, x, y: put(stage_ref.at[at], x, y),
    )
    for copy in copies:
        copy.wait()


def grant(mebibytes):
    return pltpu.CompilerParams(vmem_limit_bytes=mebibytes << 20)


def takes(microseconds):
    return pl.CostEstimate(
        flops=0, bytes_accessed=int(microseconds * 3_000_000), transcendentals=0
    )


def in_hbm(array):
    return pltpu.with_memory_space_constraint(array, pltpu.HBM)


VMEM = pl.BlockSpec(memory_space=pltpu.VMEM)
HBM = pl.BlockSpec(memory_space=pltpu.HBM)
ANY = pl.BlockSpec(memory_space=pl.ANY)
SMEM = pl.BlockSpec(memory_space=pltpu.SMEM)


def shaped(*shape, dtype=F32):
    return jax.ShapeDtypeStruct(shape, dtype)


def eights(rows):
    return 8 * pl.cdiv(rows, 8)


def on_device(tracers, weights, offsets, owner, codes, matrix):
    cols, rows, levels, lanes = tracers.shape
    width = HALO * levels
    count, ends = lax.axis_size("gx"), lax.axis_size("gy")
    axes = ("gx", "gy")
    cells = tracers.reshape(cols, rows * levels, lanes)
    partner = [(i, i ^ 1) for i in range(count)]
    across = [(i, (i + 1) % count if i % 2 else (i - 1) % count) for i in range(count)]
    first_swap = [(i * ends + j, i * ends + (j ^ 1)) for i in range(count) for j in range(ends)]
    second_swap = []
    for i in range(count):
        for j in range(ends):
            if j in (0, ends - 1):
                second_swap.append((i * ends + j, (i + count // 2) % count * ends + j))
            else:
                second_swap.append((i * ends + j, i * ends + (j + 1 if j % 2 else j - 1)))

    deep = eights(width)
    strip, corner = width * cols, 2 * width * HALO
    columns = shaped(HALO, rows * levels, lanes)
    edges, message, outer = pl.pallas_call(
        pack_kernel,
        out_shape=(shaped(2 * strip, lanes), shaped(eights(strip + corner), lanes), columns),
        in_specs=[HBM],
        out_specs=(VMEM, VMEM, VMEM),
        scratch_shapes=[
            pltpu.VMEM((cols, deep, lanes), F32),
            pltpu.VMEM((cols, deep, lanes), F32),
            pltpu.SemaphoreType.DMA((3,)),
        ],
        name="pack",
        compiler_params=grant(4),
        cost_estimate=takes(1.0),
    )(in_hbm(cells))
    got = lax.ppermute(message, "gx", across)
    outer_got = lax.ppermute(outer, "gx", across)

    field_rows = eights((LEAD + rows + HALO + PITCH - BLOCK_Y - 2 * HALO) * levels)
    field_shape = shaped(cols + 2 * HALO, field_rows, lanes)
    run = 4
    held = max(run, count // 2)
    weights = jnp.swapaxes(weights, 1, 2)
    offsets = jnp.swapaxes(offsets, 1, 2)
    load = pl.pallas_call(
        functools.partial(load_kernel, count, ends, held),
        out_shape=(
            shaped(8, lanes, dtype=jnp.int32),
            columns,
            shaped(*weights.shape),
            shaped(*offsets.shape, dtype=jnp.int32),
            shaped(*matrix.shape, dtype=BF16),
            field_shape,
        ),
        in_specs=[HBM] * 6 + [ANY],
        out_specs=(VMEM,) * 6,
        scratch_shapes=[
            pltpu.SMEM(owner.shape, jnp.int32),
            pltpu.SMEM(codes.shape, jnp.int32),
            pltpu.SemaphoreType.DMA((6 + cols // BLOCK_X,)),
        ],
        name="load",
        compiler_params=grant(4),
        cost_estimate=takes(1.0),
    )
    table, inner, weights, offsets, matrix, field = load(
        *[in_hbm(a) for a in (owner, codes, cells, weights, offsets, matrix)], message
    )

    x_blocks, y_blocks = cols // BLOCK_X, rows // BLOCK_Y

    def band_of(block, after):
        return pl.pallas_call(
            functools.partial(band_kernel, levels, rows, block),
            out_shape=shaped(y_blocks * levels, 2 * BLOCK_X * BLOCK_Y, 2 * LANES, dtype=BF16),
            in_specs=[VMEM] * 3 + [ANY],
            out_specs=VMEM,
            name="band",
            compiler_params=grant(4),
            cost_estimate=takes(0.5),
        )(weights, offsets, matrix, after)

    relay, first = pl.pallas_call(
        functools.partial(relay_kernel, cols, width),
        out_shape=(
            shaped(eights(corner + 2 * strip), lanes),
            shaped(eights(width * (cols + HALO)), lanes),
        ),
        in_specs=[VMEM] * 3 + [ANY],
        out_specs=(VMEM, VMEM),
        name="relay",
        compiler_params=grant(2),
        cost_estimate=takes(0.5),
    )(edges, message, got, table)
    other = lax.ppermute(relay, "gx", partner)
    first_got = lax.ppermute(first, axes, first_swap)
    inner_got = lax.ppermute(inner, "gx", partner)

    ring = pl.pallas_call(
        functools.partial(join_kernel, cols, width),
        out_shape=shaped(run * strip, lanes),
        in_specs=[VMEM] * 3 + [ANY],
        out_specs=VMEM,
        name="join",
        compiler_params=grant(2),
        cost_estimate=takes(0.5),
    )(message, got, other, relay)
    while run < held:
        shift = run
        more = lax.ppermute(ring, "gx", [((i + shift) % count, i) for i in range(count)])
        ring = jnp.concatenate([ring, more])
        run *= 2

    z_rows = eights(width * (cols + 2 * HALO))
    second = pl.pallas_call(
        functools.partial(rows_kernel, cols, width, count, ends, run),
        out_shape=shaped(z_rows, lanes),
        in_specs=[VMEM] * 5,
        out_specs=VMEM,
        name="rows",
        cost_estimate=takes(1.0),
        compiler_params=grant(2 * pl.cdiv(run, 8)),
    )(table, edges, other, got, ring)
    second_got = lax.ppermute(second, axes, second_swap)

    bands = [band_of(block, second) for block in range(x_blocks)]

    turned = pl.pallas_call(
        functools.partial(turn_kernel, cols, width),
        out_shape=shaped(eights(width * HALO), lanes),
        in_specs=[VMEM] + [ANY] * x_blocks,
        out_specs=VMEM,
        name="turn",
        compiler_params=grant(2),
        cost_estimate=takes(0.1),
    )(first_got, *bands)
    turned_got = lax.ppermute(turned, "gx", partner)
    inside = [(x, y) for y in range(1, y_blocks - 1) for x in range(x_blocks)]
    edge = [(x, y) for y in (0, y_blocks - 1) for x in range(x_blocks)]
    block_shape = (BLOCK_X, BLOCK_Y * levels, lanes)
    middle = pl.pallas_call(
        functools.partial(middle_kernel, levels, inside),
        out_shape=(field_shape, shaped(len(inside), *block_shape)),
        in_specs=[VMEM, VMEM, ANY] + [VMEM] * (1 + x_blocks),
        out_specs=(VMEM, VMEM),
        input_output_aliases={3: 0},
        name="middle",
        cost_estimate=takes(0.7),
        compiler_params=grant(6),
    )
    field, done = middle(inner_got, outer_got, second, field, *bands)
    _, updated = pl.pallas_call(
        functools.partial(
            edge_kernel, levels, cols, rows * levels, count, ends, run, edge, inside
        ),
        out_shape=(field_shape, shaped(cols, rows * levels, lanes)),
        in_specs=[VMEM] * (7 + x_blocks),
        out_specs=(VMEM, HBM),
        scratch_shapes=[
            pltpu.VMEM((len(edge), *block_shape), F32),
            pltpu.SemaphoreType.DMA((len(edge) + len(inside),)),
        ],
        input_output_aliases={6: 0},
        name="edge",
        cost_estimate=takes(1.0),
        compiler_params=grant(6),
    )(table, first_got, turned_got, second_got, ring, done, field, *bands)
    return updated.reshape(cols, rows, levels, lanes)


def solution(mesh):
    split = P("gx", "gy", None, None)
    in_specs = (split, P("gx", "gy", None), P("gx", "gy", None), P(), P(), P())


    def run(tracers, weights, offsets, owner, codes):
        matrix = jnp.asarray(spread_matrix(tracers.shape[2]), BF16)
        body = jax.shard_map(
            on_device, mesh=mesh, in_specs=in_specs, out_specs=split, check_vma=False
        )
        return body(tracers, weights, offsets, owner, codes, matrix)

    return run
```

```python
import functools

import jax
import jax.numpy as jnp
import numpy as np
from jax import lax
from jax.experimental import pallas as pl
from jax.experimental.pallas import tpu as pltpu
from jax.sharding import PartitionSpec as P

HALO = 3
BLOCK_X = 4
BLOCK_Y = 16
PITCH = 24
LANES = 128
LEAD = 4
BF16 = jnp.bfloat16
F32 = jnp.float32

STENCILS = [
    {(0, 0): 1.0},
    {(1, 0): 0.5, (-1, 0): -0.5},
    {(0, 1): 0.5, (0, -1): -0.5},
    {(1, 0): 0.5, (0, 0): -1.0, (-1, 0): 0.5},
    {(0, 1): 0.5, (0, 0): -1.0, (0, -1): 0.5},
    {(1, 1): 0.25, (1, -1): -0.25, (-1, 1): -0.25, (-1, -1): 0.25},
]


def spread_matrix(levels):
    terms = 24 * levels
    rows = 2 * terms + 8 * pl.cdiv(2 * levels, 8)
    matrix = np.zeros((rows, 2 * levels * LANES), np.float32)
    for level in range(levels):
        for piece in range(4):
            for moment, stencil in enumerate(STENCILS):
                for (east, north), value in stencil.items():
                    lane = (piece // 2 + 1 + east) * PITCH + piece % 2 + 1 + north
                    row = 24 * level + 6 * piece + moment
                    matrix[row, level * LANES + lane] += value
                    matrix[terms + row, level * LANES + lane] += value
        first = (levels + level) * LANES
        matrix[2 * terms + 2 * level, first : first + LANES] = PITCH
        matrix[2 * terms + 2 * level + 1, first : first + LANES] = 1
    return matrix


def load_kernel(count, ends, run, owner_ref, codes_ref, cells_ref, weights_ref, offsets_ref,
                matrix_ref, after_ref, table_ref, inner_ref, weights_out, offsets_out, matrix_out,
                field_ref, owner, codes, sems):
    del after_ref
    index, place = lax.axis_index("gx"), lax.axis_index("gy")
    cols, rows, _ = cells_ref.shape
    lead = LEAD * (weights_ref.shape[1] // 24)
    last = cols - HALO
    pairs = [
        (owner_ref, owner),
        (codes_ref, codes),
        (cells_ref.at[pl.ds(jnp.where(index % 2 == 0, last, 0), HALO)], inner_ref),
        (weights_ref, weights_out),
        (offsets_ref, offsets_out),
        (matrix_ref, matrix_out),
    ]
    for col in range(0, cols, BLOCK_X):
        to = field_ref.at[pl.ds(HALO + col, BLOCK_X), pl.ds(lead, rows)]
        pairs.append((cells_ref.at[pl.ds(col, BLOCK_X)], to))
    copies = [pltpu.make_async_copy(a, b, sems.at[at]) for at, (a, b) in enumerate(pairs)]
    for copy in copies:
        copy.start()
    copies[0].wait()
    copies[1].wait()
    side = jnp.where(place == 0, 0, 1)
    window = Window(cells_ref.shape[0], 0, count, run, None)
    target = lax.rem(index + count // 2, count)
    is_end = jnp.logical_or(place == 0, place == ends - 1)
    code = jnp.where(is_end, codes[side, index], 0)
    lines = [window.start(owner[side, target]), window.start(owner[side, index]), code]
    for at, line in enumerate(lines):
        table_ref[at : at + 1] = jnp.full((1, LANES), line, jnp.int32)
    for copy in copies[2:]:
        copy.wait()


def band_kernel(levels, rows, block, weights_ref, offsets_ref, matrix_ref, after_ref, band_ref):
    del after_ref
    y_blocks = rows // BLOCK_Y
    lane = lax.broadcasted_iota(jnp.int32, (rows, LANES), 1)
    row_in = lax.broadcasted_iota(jnp.int32, (rows, LANES), 0) % BLOCK_Y
    base = lane - row_in - 2 * PITCH - 2
    pad = matrix_ref.shape[0] - 2 * weights_ref.shape[1] - offsets_ref.shape[1]

    def column(x):
        weights = weights_ref[x]
        high = weights.astype(BF16).astype(F32)
        stacked = jnp.concatenate(
            [high, weights - high, offsets_ref[x].astype(F32), jnp.zeros((pad, rows), F32)], axis=0
        ).astype(BF16)
        spread = lax.dot_general(
            stacked, matrix_ref[...], (((0,), (0,)), ((), ())), preferred_element_type=F32
        )
        inner = x % BLOCK_X
        at = inner * BLOCK_Y
        low = at + BLOCK_X * BLOCK_Y
        for level in range(levels):
            points = spread[:, level * LANES : (level + 1) * LANES]
            first = (levels + level) * LANES
            shift = spread[:, first : first + LANES].astype(jnp.int32)
            for y in range(y_blocks):
                mine = slice(y * BLOCK_Y, (y + 1) * BLOCK_Y)
                index = base[mine] - shift[mine] - inner * PITCH
                picked = jnp.take_along_axis(
                    points[mine], index & (LANES - 1), axis=1, mode="promise_in_bounds"
                )
                top = picked.astype(BF16).astype(F32)
                rest = picked - top
                here = index >= 0
                slot = y * levels + level
                for part in range(2):
                    lanes = slice(part * LANES, (part + 1) * LANES)
                    keep = here if part == 0 else jnp.logical_not(here)
                    band_ref[slot, at : at + BLOCK_Y, lanes] = jnp.where(keep, top, 0.0).astype(BF16)
                    band_ref[slot, low : low + BLOCK_Y, lanes] = jnp.where(keep, rest, 0.0).astype(BF16)

    for step in range(BLOCK_X):
        column(block * BLOCK_X + step)


def pack_kernel(ends, cells_ref, edges_ref, message_ref, outer_ref, low_ref, high_ref, sems):
    cols, rows, _ = cells_ref.shape
    width = edges_ref.shape[0] // cols // 2
    deep = low_ref.shape[1]
    even, place = lax.axis_index("gx") % 2 == 0, lax.axis_index("gy")
    low, up = place == 0, place % 2 == 0
    is_end = jnp.logical_or(low, place == ends - 1)
    last = cols - HALO
    copies = [
        pltpu.make_async_copy(cells_ref.at[:, pl.ds(0, deep)], low_ref, sems.at[0]),
        pltpu.make_async_copy(cells_ref.at[:, pl.ds(rows - deep, deep)], high_ref, sems.at[1]),
        pltpu.make_async_copy(
            cells_ref.at[pl.ds(jnp.where(even, 0, last), HALO)], outer_ref, sems.at[2]
        ),
    ]
    for copy in copies:
        copy.start()
    for copy in copies[:2]:
        copy.wait()
    for col in range(cols):
        at = 2 * width * col
        bottom, top = low_ref[col, :width], high_ref[col, deep - width :]
        edges_ref[at : at + width] = bottom
        edges_ref[at + width : at + 2 * width] = top
        strip = jnp.where(low, bottom, top)
        if col < HALO:
            bottom = jnp.where(even, bottom, low_ref[last + col, :width])
            top = jnp.where(even, top, high_ref[last + col, deep - width :])
            message_ref[width * col : width * (col + 1)] = jnp.where(up, top, bottom)
            strip = jnp.where(is_end, strip, jnp.where(up, bottom, top))
        to = width * (HALO + col)
        message_ref[to : to + width] = strip
    clear(message_ref, width * (HALO + cols))
    copies[2].wait()


def clear(ref, at):
    if at < ref.shape[0]:
        ref[at:] = jnp.zeros((ref.shape[0] - at, LANES), F32)


def relay_kernel(cols, width, ends, edges_ref, message_ref, got_ref, after_ref, relay_ref,
                 first_ref):
    del after_ref
    even, place = lax.axis_index("gx") % 2 == 0, lax.axis_index("gy")
    up = place % 2 == 0
    is_end = jnp.logical_or(place == 0, place == ends - 1)
    corner, strip = width * HALO, width * cols
    relay_ref[:strip] = message_ref[corner : corner + strip]
    relay_ref[strip : 2 * strip] = got_ref[corner : corner + strip]
    for col in range(HALO):
        left, right = 2 * width * col, 2 * width * (cols - HALO + col)
        low = jnp.where(even, edges_ref[right : right + width], edges_ref[left : left + width])
        left, right = left + width, right + width
        high = jnp.where(even, edges_ref[right : right + width], edges_ref[left : left + width])
        to = slice(width * col, width * (col + 1))
        relay_ref[to] = jnp.where(is_end, relay_ref[to], jnp.where(up, low, high))
    clear(relay_ref, 2 * strip)
    first_ref[:corner] = got_ref[:corner]
    for col in range(cols):
        at = 2 * width * col
        to = corner + width * col
        first_ref[to : to + width] = jnp.where(
            up, edges_ref[at + width : at + 2 * width], edges_ref[at : at + width]
        )
    clear(first_ref, corner + strip)


def turn_kernel(levels, cols, width, count, ends, run, first_ref, *refs):
    run_ref, table_ref, corner_ref, glued_ref, mask_ref = refs[-5:]
    even, place = lax.axis_index("gx") % 2 == 0, lax.axis_index("gy")
    size = HALO * width
    last = (HALO + cols) * width
    corner_ref[:size] = jnp.where(even, first_ref[last - size : last], first_ref[size : 2 * size])
    clear(corner_ref, size)
    wide = cols + 2 * HALO
    window = Window(cols, width, count, run, run_ref)
    start, code = table_ref[1:2, 0:1][0, 0], table_ref[2:3, 0:1][0, 0]
    is_end = jnp.logical_or(place == 0, place == ends - 1)
    mirrored, flipped = code % 2 == 1, code // 2 % 2 == 1
    for u in range(wide):
        to = slice(width * u, width * (u + 1))
        held, strip = window.column(start, jnp.where(mirrored, wide - 1 - u, u))
        glued_ref[to] = jnp.where(flipped, turn_rows(strip, levels), strip)
        mask_ref[to] = jnp.full(
            (width, LANES), jnp.where(jnp.logical_and(is_end, held), 1.0, 0.0), F32
        )
    clear(glued_ref, wide * width)
    clear(mask_ref, wide * width)


def turn_rows(strip, levels):
    return jnp.concatenate(
        [strip[levels * r : levels * (r + 1)] for r in reversed(range(HALO))], axis=0
    )


def join_kernel(cols, width, message_ref, got_ref, other_ref, after_ref, run_ref):
    del after_ref
    even = lax.axis_index("gx") % 2 == 0
    corner, strip = width * HALO, width * cols
    mine, far = message_ref[corner : corner + strip], got_ref[corner : corner + strip]
    near, beyond = other_ref[:strip], other_ref[strip : 2 * strip]
    pairs = ((far, beyond), (mine, near), (near, mine), (beyond, far))
    for at, (a, b) in enumerate(pairs):
        run_ref[at * strip : (at + 1) * strip] = jnp.where(even, a, b)


class Window:
    def __init__(self, cols, width, count, run, held):
        self.cols, self.width, self.total, self.run = cols, width, count * cols, run
        self.held = held
        index = lax.axis_index("gx")
        self.first = index - index % 2 - 1

    def start(self, owner):
        return lax.rem((owner - self.first) * self.cols - HALO + 2 * self.total, self.total)

    def column(self, start, step):
        at = start + step
        at = jnp.where(at >= self.total, at - self.total, at)
        row = jnp.minimum(at, self.run * self.cols - 1) * self.width
        return at < self.run * self.cols, self.held[pl.ds(row, self.width)]


def rows_kernel(cols, width, count, ends, run, table_ref, edges_ref, other_ref, got_ref, run_ref,
                second_ref):
    even, place = lax.axis_index("gx") % 2 == 0, lax.axis_index("gy")
    top = place % 2 == 1

    def column(u):
        if HALO <= u < HALO + cols:
            at = 2 * width * (u - HALO)
            return jnp.where(
                top, edges_ref[at + width : at + 2 * width], edges_ref[at : at + width]
            )
        col = u if u < HALO else u - HALO - cols
        near = other_ref[width * col : width * (col + 1)]
        far = got_ref[width * (HALO + col) : width * (HALO + col + 1)]
        return jnp.where(even == (u < HALO), far, near)

    wide = cols + 2 * HALO
    window = Window(cols, width, count, run, run_ref)
    start = table_ref[0:1, 0:1][0, 0]
    is_end = jnp.logical_or(place == 0, place == ends - 1)
    for u in range(wide):
        to = slice(u * width, (u + 1) * width)
        _, glued = window.column(start, u)
        second_ref[to] = jnp.where(is_end, glued, column(u))
    clear(second_ref, wide * width)


def block_sum(field_ref, bands, x, y, levels, level):
    size = BLOCK_X * BLOCK_Y
    reach = BLOCK_X + 2 * HALO
    begin = (y * BLOCK_Y + LEAD - HALO) * levels + level
    points = jnp.concatenate(
        [
            field_ref[x * BLOCK_X + c, pl.ds(begin, PITCH, stride=levels), :]
            for c in range(reach)
        ]
        + [jnp.zeros((2 * LANES - reach * PITCH, LANES), F32)],
        axis=0,
    )
    top = points.astype(BF16)
    rest = (points - top.astype(F32)).astype(BF16)
    band = bands[x][y * levels + level]
    product = jnp.dot(band, jnp.concatenate([top, rest], axis=1), preferred_element_type=F32)
    return product[:size, :LANES] + (product[:size, LANES:] + product[size:, :LANES])


def remap_blocks(field_ref, bands, stage_ref, levels, blocks, ready=None):
    for at, (x, y) in enumerate(blocks):
        for level in range(levels):
            total = block_sum(field_ref, bands, x, y, levels, level)
            for c in range(BLOCK_X):
                stage_ref[at, c, pl.ds(level, BLOCK_Y, stride=levels), :] = total[
                    c * BLOCK_Y : (c + 1) * BLOCK_Y
                ]
        if ready is not None:
            ready(at, x, y)


def middle_kernel(levels, blocks, inner_ref, outer_ref, after_ref, field_in, *refs):
    del after_ref, field_in
    *bands, field_ref, stage_ref = refs
    rows, wide = inner_ref.shape[1], field_ref.shape[0]
    lead = LEAD * levels
    even = lax.axis_index("gx") % 2 == 0
    for col in range(HALO):
        inner, outer = inner_ref[col], outer_ref[col]
        field_ref[col, lead : lead + rows] = jnp.where(even, outer, inner)
        field_ref[wide - HALO + col, lead : lead + rows] = jnp.where(even, inner, outer)
    remap_blocks(field_ref, bands, stage_ref, levels, blocks)


def put_block(source, out_ref, sem, x, y):
    _, deep, _ = source.shape
    to = out_ref.at[pl.ds(x * BLOCK_X, BLOCK_X), pl.ds(pl.multiple_of(y * deep, deep), deep)]
    copy = pltpu.make_async_copy(source, to, sem)
    copy.start()
    return copy


def near_kernel(levels, cols, rows, first_ref, corner_ref, field_in, *refs):
    del field_in
    *bands, field_ref, stage_ref = refs
    width, lead = HALO * levels, LEAD * levels
    even, up = lax.axis_index("gx") % 2 == 0, lax.axis_index("gy") % 2 == 0
    tail = field_ref.shape[1] - lead - rows - width
    for u in range(cols + 2 * HALO):
        if HALO <= u < HALO + cols:
            strip = first_ref[u * width : (u + 1) * width]
        else:
            col = u if u < HALO else u - HALO - cols
            far = first_ref[col * width : (col + 1) * width]
            near = corner_ref[col * width : (col + 1) * width]
            strip = jnp.where(even == (u < HALO), far, near)
        field_ref[u, lead - width : lead] = strip
        field_ref[u, lead + rows : lead + rows + width] = strip
        field_ref[u, lead + rows + width :] = jnp.zeros((tail, LANES), F32)
    last = rows // levels // BLOCK_Y - 1
    blocks = [(x, jnp.where(up, last, 0)) for x in range(cols // BLOCK_X)]
    remap_blocks(field_ref, bands, stage_ref, levels, blocks)


def edge_kernel(levels, cols, rows, done, table_ref, second_ref, glued_ref, mask_ref, near_ref,
                done_ref, field_in, *refs):
    del field_in
    *bands, field_ref, out_ref, stage_ref, sems = refs
    last = rows // levels // BLOCK_Y - 1
    up = lax.axis_index("gy") % 2 == 0
    blocks = [(x, jnp.where(up, 0, last)) for x in range(cols // BLOCK_X)]
    copies = []
    ready = [(done_ref.at[at], x, y) for at, (x, y) in enumerate(done)]
    ready += [(near_ref.at[x], x, last - y) for x, y in blocks]
    for source, x, y in ready:
        copies.append(put_block(source, out_ref, sems.at[len(copies)], x, y))

    def put(at, x, y):
        copies.append(put_block(stage_ref.at[at], out_ref, sems.at[len(copies)], x, y))

    width, lead = HALO * levels, LEAD * levels
    wide = cols + 2 * HALO
    code = table_ref[2:3, 0:1][0, 0]
    mirrored, flipped = code % 2 == 1, code // 2 % 2 == 1
    for u in range(wide):
        to = slice(width * u, width * (u + 1))
        back = slice(width * (wide - 1 - u), width * (wide - u))
        come = jnp.where(mirrored, second_ref[back], second_ref[to])
        come = jnp.where(flipped, turn_rows(come, levels), come)
        strip = jnp.where(mask_ref[to] > 0, glued_ref[to], come)
        for at, mine in ((lead - width, up), (lead + rows, jnp.logical_not(up))):
            old = field_ref[u, at : at + width]
            field_ref[u, at : at + width] = jnp.where(mine, strip, old)
    remap_blocks(field_ref, bands, stage_ref, levels, blocks, put)
    for copy in copies:
        copy.wait()


def grant(mebibytes):
    return pltpu.CompilerParams(vmem_limit_bytes=mebibytes << 20)


def takes(microseconds):
    return pl.CostEstimate(
        flops=0, bytes_accessed=int(microseconds * 3_000_000), transcendentals=0
    )


def in_hbm(array):
    return pltpu.with_memory_space_constraint(array, pltpu.HBM)


VMEM = pl.BlockSpec(memory_space=pltpu.VMEM)
HBM = pl.BlockSpec(memory_space=pltpu.HBM)
ANY = pl.BlockSpec(memory_space=pl.ANY)
SMEM = pl.BlockSpec(memory_space=pltpu.SMEM)


def shaped(*shape, dtype=F32):
    return jax.ShapeDtypeStruct(shape, dtype)


def eights(rows):
    return 8 * pl.cdiv(rows, 8)


def on_device(tracers, weights, offsets, owner, codes, matrix):
    cols, rows, levels, lanes = tracers.shape
    width = HALO * levels
    count, ends = lax.axis_size("gx"), lax.axis_size("gy")
    axes = ("gx", "gy")
    cells = tracers.reshape(cols, rows * levels, lanes)
    partner = [(i, i ^ 1) for i in range(count)]
    across = [(i, (i + 1) % count if i % 2 else (i - 1) % count) for i in range(count)]
    first_swap = [(i * ends + j, i * ends + (j ^ 1)) for i in range(count) for j in range(ends)]
    second_swap = []
    for i in range(count):
        for j in range(ends):
            if j in (0, ends - 1):
                second_swap.append((i * ends + j, (i + count // 2) % count * ends + j))
            else:
                second_swap.append((i * ends + j, i * ends + (j + 1 if j % 2 else j - 1)))

    deep = eights(width)
    strip, corner = width * cols, width * HALO
    columns = shaped(HALO, rows * levels, lanes)
    edges, message, outer = pl.pallas_call(
        functools.partial(pack_kernel, ends),
        out_shape=(shaped(2 * strip, lanes), shaped(eights(strip + corner), lanes), columns),
        in_specs=[HBM],
        out_specs=(VMEM, VMEM, VMEM),
        scratch_shapes=[
            pltpu.VMEM((cols, deep, lanes), F32),
            pltpu.VMEM((cols, deep, lanes), F32),
            pltpu.SemaphoreType.DMA((3,)),
        ],
        name="pack",
        compiler_params=grant(4),
        cost_estimate=takes(1.0),
    )(in_hbm(cells))
    got = lax.ppermute(message, "gx", across)
    outer_got = lax.ppermute(outer, "gx", across)

    field_rows = eights((LEAD + rows + HALO + PITCH - BLOCK_Y - 2 * HALO) * levels)
    field_shape = shaped(cols + 2 * HALO, field_rows, lanes)
    run = 4
    held = max(run, count // 2)
    weights = jnp.swapaxes(weights, 1, 2)
    offsets = jnp.swapaxes(offsets, 1, 2)
    load = pl.pallas_call(
        functools.partial(load_kernel, count, ends, held),
        out_shape=(
            shaped(8, lanes, dtype=jnp.int32),
            columns,
            shaped(*weights.shape),
            shaped(*offsets.shape, dtype=jnp.int32),
            shaped(*matrix.shape, dtype=BF16),
            field_shape,
        ),
        in_specs=[HBM] * 6 + [ANY],
        out_specs=(VMEM,) * 6,
        scratch_shapes=[
            pltpu.SMEM(owner.shape, jnp.int32),
            pltpu.SMEM(codes.shape, jnp.int32),
            pltpu.SemaphoreType.DMA((6 + cols // BLOCK_X,)),
        ],
        name="load",
        compiler_params=grant(4),
        cost_estimate=takes(1.0),
    )
    table, inner, weights, offsets, matrix, field = load(
        *[in_hbm(a) for a in (owner, codes, cells, weights, offsets, matrix)], message
    )

    x_blocks, y_blocks = cols // BLOCK_X, rows // BLOCK_Y

    def band_of(block, after):
        return pl.pallas_call(
            functools.partial(band_kernel, levels, rows, block),
            out_shape=shaped(y_blocks * levels, 2 * BLOCK_X * BLOCK_Y, 2 * LANES, dtype=BF16),
            in_specs=[VMEM] * 3 + [ANY],
            out_specs=VMEM,
            name="band",
            compiler_params=grant(4),
            cost_estimate=takes(0.5),
        )(weights, offsets, matrix, after)

    bands = [band_of(0, table)]
    relay, first = pl.pallas_call(
        functools.partial(relay_kernel, cols, width, ends),
        out_shape=(
            shaped(eights(2 * strip), lanes),
            shaped(eights(width * (cols + HALO)), lanes),
        ),
        in_specs=[VMEM] * 3 + [ANY],
        out_specs=(VMEM, VMEM),
        name="relay",
        compiler_params=grant(2),
        cost_estimate=takes(0.5),
    )(edges, message, got, bands[0])
    other = lax.ppermute(relay, "gx", partner)
    first_got = lax.ppermute(first, axes, first_swap)
    inner_got = lax.ppermute(inner, "gx", partner)

    ring = pl.pallas_call(
        functools.partial(join_kernel, cols, width),
        out_shape=shaped(run * strip, lanes),
        in_specs=[VMEM] * 3 + [ANY],
        out_specs=VMEM,
        name="join",
        compiler_params=grant(2),
        cost_estimate=takes(0.5),
    )(message, got, other, relay)
    while run < held:
        shift = run
        more = lax.ppermute(ring, "gx", [((i + shift) % count, i) for i in range(count)])
        ring = jnp.concatenate([ring, more])
        run *= 2

    z_rows = eights(width * (cols + 2 * HALO))
    second = pl.pallas_call(
        functools.partial(rows_kernel, cols, width, count, ends, run),
        out_shape=shaped(z_rows, lanes),
        in_specs=[VMEM] * 5,
        out_specs=VMEM,
        name="rows",
        cost_estimate=takes(1.0),
        compiler_params=grant(2 * pl.cdiv(run, 8)),
    )(table, edges, other, got, ring)
    second_got = lax.ppermute(second, axes, second_swap)

    bands.extend(band_of(block, second) for block in range(1, x_blocks))

    turned, glued, mask = pl.pallas_call(
        functools.partial(turn_kernel, levels, cols, width, count, ends, run),
        out_shape=(shaped(eights(width * HALO), lanes), shaped(z_rows, lanes), shaped(z_rows, lanes)),
        in_specs=[VMEM] + [ANY] * x_blocks + [VMEM] * 2,
        out_specs=(VMEM, VMEM, VMEM),
        name="turn",
        compiler_params=grant(2),
        cost_estimate=takes(0.1),
    )(first_got, *bands, ring, table)
    turned_got = lax.ppermute(turned, "gx", partner)
    inside = [(x, y) for y in range(1, y_blocks - 1) for x in range(x_blocks)]
    block_shape = (BLOCK_X, BLOCK_Y * levels, lanes)
    middle = pl.pallas_call(
        functools.partial(middle_kernel, levels, inside),
        out_shape=(field_shape, shaped(len(inside), *block_shape)),
        in_specs=[VMEM, VMEM, ANY] + [VMEM] * (1 + x_blocks),
        out_specs=(VMEM, VMEM),
        input_output_aliases={3: 0},
        name="middle",
        cost_estimate=takes(0.7),
        compiler_params=grant(6),
    )
    field, done = middle(inner_got, outer_got, second, field, *bands)
    out_shape = shaped(cols, rows * levels, lanes)
    field, near = pl.pallas_call(
        functools.partial(near_kernel, levels, cols, rows * levels),
        out_shape=(field_shape, shaped(x_blocks, *block_shape)),
        in_specs=[VMEM] * (3 + x_blocks),
        out_specs=(VMEM, VMEM),
        input_output_aliases={2: 0},
        name="near",
        cost_estimate=takes(0.5),
        compiler_params=grant(6),
    )(first_got, turned_got, field, *bands)
    _, updated = pl.pallas_call(
        functools.partial(edge_kernel, levels, cols, rows * levels, inside),
        out_shape=(field_shape, out_shape),
        in_specs=[VMEM] * (7 + x_blocks),
        out_specs=(VMEM, HBM),
        scratch_shapes=[
            pltpu.VMEM((x_blocks, *block_shape), F32),
            pltpu.SemaphoreType.DMA((2 * x_blocks + len(inside),)),
        ],
        input_output_aliases={6: 0},
        name="edge",
        cost_estimate=takes(1.0),
        compiler_params=grant(6),
    )(table, second_got, glued, mask, near, done, field, *bands)
    return updated.reshape(cols, rows, levels, lanes)


def solution(mesh):
    split = P("gx", "gy", None, None)
    in_specs = (split, P("gx", "gy", None), P("gx", "gy", None), P(), P(), P())


    def run(tracers, weights, offsets, owner, codes):
        matrix = jnp.asarray(spread_matrix(tracers.shape[2]), BF16)
        body = jax.shard_map(
            on_device, mesh=mesh, in_specs=in_specs, out_specs=split, check_vma=False
        )
        return body(tracers, weights, offsets, owner, codes, matrix)

    return run
```

```python
import functools

import jax
import jax.numpy as jnp
import numpy as np
from jax import lax
from jax.experimental import pallas as pl
from jax.experimental.pallas import tpu as pltpu
from jax.sharding import PartitionSpec as P

HALO = 3
BLOCK_X = 4
BLOCK_Y = 16
PITCH = 24
LANES = 128
LEAD = 4
BF16 = jnp.bfloat16
F32 = jnp.float32

STENCILS = [
    {(0, 0): 1.0},
    {(1, 0): 0.5, (-1, 0): -0.5},
    {(0, 1): 0.5, (0, -1): -0.5},
    {(1, 0): 0.5, (0, 0): -1.0, (-1, 0): 0.5},
    {(0, 1): 0.5, (0, 0): -1.0, (0, -1): 0.5},
    {(1, 1): 0.25, (1, -1): -0.25, (-1, 1): -0.25, (-1, -1): 0.25},
]


def spread_matrix(levels):
    terms = 24 * levels
    rows = 2 * terms + 8 * pl.cdiv(2 * levels, 8)
    matrix = np.zeros((rows, 2 * levels * LANES), np.float32)
    for level in range(levels):
        for piece in range(4):
            for moment, stencil in enumerate(STENCILS):
                for (east, north), value in stencil.items():
                    lane = (piece // 2 + 1 + east) * PITCH + piece % 2 + 1 + north
                    row = 24 * level + 6 * piece + moment
                    matrix[row, level * LANES + lane] += value
                    matrix[terms + row, level * LANES + lane] += value
        first = (levels + level) * LANES
        matrix[2 * terms + 2 * level, first : first + LANES] = PITCH
        matrix[2 * terms + 2 * level + 1, first : first + LANES] = 1
    return matrix


def load_kernel(count, ends, run, turns, owner_ref, codes_ref, cells_ref, weights_ref, offsets_ref,
                matrix_ref, after_ref, *refs):
    del after_ref
    table_ref, inner_ref, weights_out, offsets_out, matrix_out, field_ref, owner, codes, sems = refs[-9:]

    @pl.when(((lax.axis_index("gx") + 1) // 2 % 2 == 0) == turns)
    def _():
        index, place = lax.axis_index("gx"), lax.axis_index("gy")
        cols, rows, _ = cells_ref.shape
        lead = LEAD * (weights_ref.shape[1] // 24)
        last = cols - HALO
        pairs = [
            (owner_ref, owner),
            (codes_ref, codes),
            (cells_ref.at[pl.ds(jnp.where(index % 2 == 0, last, 0), HALO)], inner_ref),
            (weights_ref, weights_out),
            (offsets_ref, offsets_out),
            (matrix_ref, matrix_out),
        ]
        for col in range(0, cols, BLOCK_X):
            to = field_ref.at[pl.ds(HALO + col, BLOCK_X), pl.ds(lead, rows)]
            pairs.append((cells_ref.at[pl.ds(col, BLOCK_X)], to))
        copies = [pltpu.make_async_copy(a, b, sems.at[at]) for at, (a, b) in enumerate(pairs)]
        for copy in copies:
            copy.start()
        copies[0].wait()
        copies[1].wait()
        side = jnp.where(place == 0, 0, 1)
        window = Window(cells_ref.shape[0], 0, count, run, None)
        target = lax.rem(index + count // 2, count)
        is_end = jnp.logical_or(place == 0, place == ends - 1)
        code = jnp.where(is_end, codes[side, index], 0)
        lines = [window.start(owner[side, target]), window.start(owner[side, index]), code]
        for at, line in enumerate(lines):
            table_ref[at : at + 1] = jnp.full((1, LANES), line, jnp.int32)
        for copy in copies[2:]:
            copy.wait()


def band_kernel(levels, rows, block, weights_ref, offsets_ref, matrix_ref, after_ref, band_ref):
    del after_ref
    y_blocks = rows // BLOCK_Y
    lane = lax.broadcasted_iota(jnp.int32, (rows, LANES), 1)
    row_in = lax.broadcasted_iota(jnp.int32, (rows, LANES), 0) % BLOCK_Y
    base = lane - row_in - 2 * PITCH - 2
    pad = matrix_ref.shape[0] - 2 * weights_ref.shape[1] - offsets_ref.shape[1]

    def column(x):
        weights = weights_ref[x]
        high = weights.astype(BF16).astype(F32)
        stacked = jnp.concatenate(
            [high, weights - high, offsets_ref[x].astype(F32), jnp.zeros((pad, rows), F32)], axis=0
        ).astype(BF16)
        spread = lax.dot_general(
            stacked, matrix_ref[...], (((0,), (0,)), ((), ())), preferred_element_type=F32
        )
        inner = x % BLOCK_X
        at = inner * BLOCK_Y
        low = at + BLOCK_X * BLOCK_Y
        for level in range(levels):
            points = spread[:, level * LANES : (level + 1) * LANES]
            first = (levels + level) * LANES
            shift = spread[:, first : first + LANES].astype(jnp.int32)
            for y in range(y_blocks):
                mine = slice(y * BLOCK_Y, (y + 1) * BLOCK_Y)
                index = base[mine] - shift[mine] - inner * PITCH
                picked = jnp.take_along_axis(
                    points[mine], index & (LANES - 1), axis=1, mode="promise_in_bounds"
                )
                top = picked.astype(BF16).astype(F32)
                rest = picked - top
                here = index >= 0
                slot = y * levels + level
                for part in range(2):
                    lanes = slice(part * LANES, (part + 1) * LANES)
                    keep = here if part == 0 else jnp.logical_not(here)
                    band_ref[slot, at : at + BLOCK_Y, lanes] = jnp.where(keep, top, 0.0).astype(BF16)
                    band_ref[slot, low : low + BLOCK_Y, lanes] = jnp.where(keep, rest, 0.0).astype(BF16)

    for step in range(BLOCK_X):
        column(block * BLOCK_X + step)


def pack_kernel(ends, cells_ref, edges_ref, message_ref, outer_ref, low_ref, high_ref, sems):
    cols, rows, _ = cells_ref.shape
    width = edges_ref.shape[0] // cols // 2
    deep = low_ref.shape[1]
    even, place = lax.axis_index("gx") % 2 == 0, lax.axis_index("gy")
    low, up = place == 0, place % 2 == 0
    is_end = jnp.logical_or(low, place == ends - 1)
    last = cols - HALO
    copies = [
        pltpu.make_async_copy(cells_ref.at[:, pl.ds(0, deep)], low_ref, sems.at[0]),
        pltpu.make_async_copy(cells_ref.at[:, pl.ds(rows - deep, deep)], high_ref, sems.at[1]),
        pltpu.make_async_copy(
            cells_ref.at[pl.ds(jnp.where(even, 0, last), HALO)], outer_ref, sems.at[2]
        ),
    ]
    for copy in copies:
        copy.start()
    for copy in copies[:2]:
        copy.wait()
    for col in range(cols):
        at = 2 * width * col
        bottom, top = low_ref[col, :width], high_ref[col, deep - width :]
        edges_ref[at : at + width] = bottom
        edges_ref[at + width : at + 2 * width] = top
        strip = jnp.where(low, bottom, top)
        if col < HALO:
            bottom = jnp.where(even, bottom, low_ref[last + col, :width])
            top = jnp.where(even, top, high_ref[last + col, deep - width :])
            message_ref[width * col : width * (col + 1)] = jnp.where(up, top, bottom)
            strip = jnp.where(is_end, strip, jnp.where(up, bottom, top))
        to = width * (HALO + col)
        message_ref[to : to + width] = strip
    clear(message_ref, width * (HALO + cols))
    copies[2].wait()


def clear(ref, at):
    if at < ref.shape[0]:
        ref[at:] = jnp.zeros((ref.shape[0] - at, LANES), F32)


def relay_kernel(cols, width, ends, edges_ref, message_ref, got_ref, after_ref, relay_ref,
                 first_ref):
    del after_ref
    even, place = lax.axis_index("gx") % 2 == 0, lax.axis_index("gy")
    up = place % 2 == 0
    is_end = jnp.logical_or(place == 0, place == ends - 1)
    corner, strip = width * HALO, width * cols
    relay_ref[:strip] = message_ref[corner : corner + strip]
    relay_ref[strip : 2 * strip] = got_ref[corner : corner + strip]
    for col in range(HALO):
        left, right = 2 * width * col, 2 * width * (cols - HALO + col)
        low = jnp.where(even, edges_ref[right : right + width], edges_ref[left : left + width])
        left, right = left + width, right + width
        high = jnp.where(even, edges_ref[right : right + width], edges_ref[left : left + width])
        to = slice(width * col, width * (col + 1))
        relay_ref[to] = jnp.where(is_end, relay_ref[to], jnp.where(up, low, high))
    clear(relay_ref, 2 * strip)
    first_ref[:corner] = got_ref[:corner]
    for col in range(cols):
        at = 2 * width * col
        to = corner + width * col
        first_ref[to : to + width] = jnp.where(
            up, edges_ref[at + width : at + 2 * width], edges_ref[at : at + width]
        )
    clear(first_ref, corner + strip)


def turn_kernel(levels, cols, width, count, ends, run, first_ref, *refs):
    run_ref, table_ref, corner_ref, glued_ref, mask_ref = refs[-5:]
    even, place = lax.axis_index("gx") % 2 == 0, lax.axis_index("gy")
    size = HALO * width
    last = (HALO + cols) * width
    corner_ref[:size] = jnp.where(even, first_ref[last - size : last], first_ref[size : 2 * size])
    clear(corner_ref, size)
    wide = cols + 2 * HALO
    window = Window(cols, width, count, run, run_ref)
    start, code = table_ref[1:2, 0:1][0, 0], table_ref[2:3, 0:1][0, 0]
    is_end = jnp.logical_or(place == 0, place == ends - 1)
    mirrored, flipped = code % 2 == 1, code // 2 % 2 == 1
    for u in range(wide):
        to = slice(width * u, width * (u + 1))
        held, strip = window.column(start, jnp.where(mirrored, wide - 1 - u, u))
        glued_ref[to] = jnp.where(flipped, turn_rows(strip, levels), strip)
        mask_ref[to] = jnp.full(
            (width, LANES), jnp.where(jnp.logical_and(is_end, held), 1.0, 0.0), F32
        )
    clear(glued_ref, wide * width)
    clear(mask_ref, wide * width)


def turn_rows(strip, levels):
    return jnp.concatenate(
        [strip[levels * r : levels * (r + 1)] for r in reversed(range(HALO))], axis=0
    )


def join_kernel(cols, width, message_ref, got_ref, other_ref, after_ref, run_ref):
    del after_ref
    even = lax.axis_index("gx") % 2 == 0
    corner, strip = width * HALO, width * cols
    mine, far = message_ref[corner : corner + strip], got_ref[corner : corner + strip]
    near, beyond = other_ref[:strip], other_ref[strip : 2 * strip]
    pairs = ((far, beyond), (mine, near), (near, mine), (beyond, far))
    for at, (a, b) in enumerate(pairs):
        run_ref[at * strip : (at + 1) * strip] = jnp.where(even, a, b)


class Window:
    def __init__(self, cols, width, count, run, held):
        self.cols, self.width, self.total, self.run = cols, width, count * cols, run
        self.held = held
        index = lax.axis_index("gx")
        self.first = index - index % 2 - 1

    def start(self, owner):
        return lax.rem((owner - self.first) * self.cols - HALO + 2 * self.total, self.total)

    def column(self, start, step):
        at = start + step
        at = jnp.where(at >= self.total, at - self.total, at)
        row = jnp.minimum(at, self.run * self.cols - 1) * self.width
        return at < self.run * self.cols, self.held[pl.ds(row, self.width)]


def rows_kernel(cols, width, count, ends, run, table_ref, edges_ref, other_ref, got_ref, run_ref,
                second_ref):
    even, place = lax.axis_index("gx") % 2 == 0, lax.axis_index("gy")
    top = place % 2 == 1

    def column(u):
        if HALO <= u < HALO + cols:
            at = 2 * width * (u - HALO)
            return jnp.where(
                top, edges_ref[at + width : at + 2 * width], edges_ref[at : at + width]
            )
        col = u if u < HALO else u - HALO - cols
        near = other_ref[width * col : width * (col + 1)]
        far = got_ref[width * (HALO + col) : width * (HALO + col + 1)]
        return jnp.where(even == (u < HALO), far, near)

    wide = cols + 2 * HALO
    window = Window(cols, width, count, run, run_ref)
    start = table_ref[0:1, 0:1][0, 0]
    is_end = jnp.logical_or(place == 0, place == ends - 1)
    for u in range(wide):
        to = slice(u * width, (u + 1) * width)
        _, glued = window.column(start, u)
        second_ref[to] = jnp.where(is_end, glued, column(u))
    clear(second_ref, wide * width)


def block_sum(field_ref, bands, x, y, levels, level):
    size = BLOCK_X * BLOCK_Y
    reach = BLOCK_X + 2 * HALO
    begin = (y * BLOCK_Y + LEAD - HALO) * levels + level
    points = jnp.concatenate(
        [
            field_ref[x * BLOCK_X + c, pl.ds(begin, PITCH, stride=levels), :]
            for c in range(reach)
        ]
        + [jnp.zeros((2 * LANES - reach * PITCH, LANES), F32)],
        axis=0,
    )
    top = points.astype(BF16)
    rest = (points - top.astype(F32)).astype(BF16)
    band = bands[x][y * levels + level]
    product = jnp.dot(band, jnp.concatenate([top, rest], axis=1), preferred_element_type=F32)
    return product[:size, :LANES] + (product[:size, LANES:] + product[size:, :LANES])


def remap_blocks(field_ref, bands, stage_ref, levels, blocks, ready=None):
    for at, (x, y) in enumerate(blocks):
        for level in range(levels):
            total = block_sum(field_ref, bands, x, y, levels, level)
            for c in range(BLOCK_X):
                stage_ref[at, c, pl.ds(level, BLOCK_Y, stride=levels), :] = total[
                    c * BLOCK_Y : (c + 1) * BLOCK_Y
                ]
        if ready is not None:
            ready(at, x, y)


def middle_kernel(levels, blocks, inner_ref, outer_ref, after_ref, field_in, *refs):
    del after_ref, field_in
    *bands, field_ref, stage_ref = refs
    rows, wide = inner_ref.shape[1], field_ref.shape[0]
    lead = LEAD * levels
    even = lax.axis_index("gx") % 2 == 0
    for col in range(HALO):
        inner, outer = inner_ref[col], outer_ref[col]
        field_ref[col, lead : lead + rows] = jnp.where(even, outer, inner)
        field_ref[wide - HALO + col, lead : lead + rows] = jnp.where(even, inner, outer)
    remap_blocks(field_ref, bands, stage_ref, levels, blocks)


def put_block(source, out_ref, sem, x, y):
    _, deep, _ = source.shape
    to = out_ref.at[pl.ds(x * BLOCK_X, BLOCK_X), pl.ds(pl.multiple_of(y * deep, deep), deep)]
    copy = pltpu.make_async_copy(source, to, sem)
    copy.start()
    return copy


def near_kernel(levels, cols, rows, first_ref, corner_ref, field_in, *refs):
    del field_in
    *bands, field_ref, stage_ref = refs
    width, lead = HALO * levels, LEAD * levels
    even, up = lax.axis_index("gx") % 2 == 0, lax.axis_index("gy") % 2 == 0
    tail = field_ref.shape[1] - lead - rows - width
    for u in range(cols + 2 * HALO):
        if HALO <= u < HALO + cols:
            strip = first_ref[u * width : (u + 1) * width]
        else:
            col = u if u < HALO else u - HALO - cols
            far = first_ref[col * width : (col + 1) * width]
            near = corner_ref[col * width : (col + 1) * width]
            strip = jnp.where(even == (u < HALO), far, near)
        field_ref[u, lead - width : lead] = strip
        field_ref[u, lead + rows : lead + rows + width] = strip
        field_ref[u, lead + rows + width :] = jnp.zeros((tail, LANES), F32)
    last = rows // levels // BLOCK_Y - 1
    blocks = [(x, jnp.where(up, last, 0)) for x in range(cols // BLOCK_X)]
    remap_blocks(field_ref, bands, stage_ref, levels, blocks)


def edge_kernel(levels, cols, rows, done, table_ref, second_ref, glued_ref, mask_ref, near_ref,
                done_ref, field_in, *refs):
    del field_in
    *bands, field_ref, out_ref, stage_ref, sems = refs
    last = rows // levels // BLOCK_Y - 1
    up = lax.axis_index("gy") % 2 == 0
    blocks = [(x, jnp.where(up, 0, last)) for x in range(cols // BLOCK_X)]
    copies = []
    ready = [(done_ref.at[at], x, y) for at, (x, y) in enumerate(done)]
    ready += [(near_ref.at[x], x, last - y) for x, y in blocks]
    for source, x, y in ready:
        copies.append(put_block(source, out_ref, sems.at[len(copies)], x, y))

    def put(at, x, y):
        copies.append(put_block(stage_ref.at[at], out_ref, sems.at[len(copies)], x, y))

    width, lead = HALO * levels, LEAD * levels
    wide = cols + 2 * HALO
    code = table_ref[2:3, 0:1][0, 0]
    mirrored, flipped = code % 2 == 1, code // 2 % 2 == 1
    for u in range(wide):
        to = slice(width * u, width * (u + 1))
        back = slice(width * (wide - 1 - u), width * (wide - u))
        come = jnp.where(mirrored, second_ref[back], second_ref[to])
        come = jnp.where(flipped, turn_rows(come, levels), come)
        strip = jnp.where(mask_ref[to] > 0, glued_ref[to], come)
        for at, mine in ((lead - width, up), (lead + rows, jnp.logical_not(up))):
            old = field_ref[u, at : at + width]
            field_ref[u, at : at + width] = jnp.where(mine, strip, old)
    remap_blocks(field_ref, bands, stage_ref, levels, blocks, put)
    for copy in copies:
        copy.wait()


def grant(mebibytes):
    return pltpu.CompilerParams(vmem_limit_bytes=mebibytes << 20)


def takes(microseconds):
    return pl.CostEstimate(
        flops=0, bytes_accessed=int(microseconds * 3_000_000), transcendentals=0
    )


def in_hbm(array):
    return pltpu.with_memory_space_constraint(array, pltpu.HBM)


VMEM = pl.BlockSpec(memory_space=pltpu.VMEM)
HBM = pl.BlockSpec(memory_space=pltpu.HBM)
ANY = pl.BlockSpec(memory_space=pl.ANY)
SMEM = pl.BlockSpec(memory_space=pltpu.SMEM)


def shaped(*shape, dtype=F32):
    return jax.ShapeDtypeStruct(shape, dtype)


def eights(rows):
    return 8 * pl.cdiv(rows, 8)


def on_device(tracers, weights, offsets, owner, codes, matrix):
    cols, rows, levels, lanes = tracers.shape
    width = HALO * levels
    count, ends = lax.axis_size("gx"), lax.axis_size("gy")
    axes = ("gx", "gy")
    cells = tracers.reshape(cols, rows * levels, lanes)
    partner = [(i, i ^ 1) for i in range(count)]
    across = [(i, (i + 1) % count if i % 2 else (i - 1) % count) for i in range(count)]
    first_swap = [(i * ends + j, i * ends + (j ^ 1)) for i in range(count) for j in range(ends)]
    second_swap = []
    for i in range(count):
        for j in range(ends):
            if j in (0, ends - 1):
                second_swap.append((i * ends + j, (i + count // 2) % count * ends + j))
            else:
                second_swap.append((i * ends + j, i * ends + (j + 1 if j % 2 else j - 1)))

    deep = eights(width)
    strip, corner = width * cols, width * HALO
    columns = shaped(HALO, rows * levels, lanes)
    edges, message, outer = pl.pallas_call(
        functools.partial(pack_kernel, ends),
        out_shape=(shaped(2 * strip, lanes), shaped(eights(strip + corner), lanes), columns),
        in_specs=[HBM],
        out_specs=(VMEM, VMEM, VMEM),
        scratch_shapes=[
            pltpu.VMEM((cols, deep, lanes), F32),
            pltpu.VMEM((cols, deep, lanes), F32),
            pltpu.SemaphoreType.DMA((3,)),
        ],
        name="pack",
        compiler_params=grant(4),
        cost_estimate=takes(1.0),
    )(in_hbm(cells))
    got = lax.ppermute(message, "gx", across)
    outer_got = lax.ppermute(outer, "gx", across)

    field_rows = eights((LEAD + rows + HALO + PITCH - BLOCK_Y - 2 * HALO) * levels)
    field_shape = shaped(cols + 2 * HALO, field_rows, lanes)
    run = 4
    held = max(run, count // 2)
    weights = jnp.swapaxes(weights, 1, 2)
    offsets = jnp.swapaxes(offsets, 1, 2)
    loaded = (
        shaped(8, lanes, dtype=jnp.int32),
        columns,
        shaped(*weights.shape),
        shaped(*offsets.shape, dtype=jnp.int32),
        shaped(*matrix.shape, dtype=BF16),
        field_shape,
    )
    sources = [in_hbm(a) for a in (owner, codes, cells, weights, offsets, matrix)] + [message]

    def load(turns, into):
        return pl.pallas_call(
            functools.partial(load_kernel, count, ends, held, turns),
            out_shape=loaded,
            in_specs=[HBM] * 6 + [ANY] + [VMEM] * len(into),
            out_specs=(VMEM,) * 6,
            scratch_shapes=[
                pltpu.SMEM(owner.shape, jnp.int32),
                pltpu.SMEM(codes.shape, jnp.int32),
                pltpu.SemaphoreType.DMA((6 + cols // BLOCK_X,)),
            ],
            input_output_aliases={7 + at: at for at in range(len(into))},
            name="load",
            compiler_params=grant(6),
            cost_estimate=takes(0.5),
        )(*sources, *into)

    parts = load(False, ())
    table, inner, weights, offsets, matrix, field = load(True, parts)

    x_blocks, y_blocks = cols // BLOCK_X, rows // BLOCK_Y

    def band_of(block, after):
        return pl.pallas_call(
            functools.partial(band_kernel, levels, rows, block),
            out_shape=shaped(y_blocks * levels, 2 * BLOCK_X * BLOCK_Y, 2 * LANES, dtype=BF16),
            in_specs=[VMEM] * 3 + [ANY],
            out_specs=VMEM,
            name="band",
            compiler_params=grant(4),
            cost_estimate=takes(0.5),
        )(weights, offsets, matrix, after)

    relay, first = pl.pallas_call(
        functools.partial(relay_kernel, cols, width, ends),
        out_shape=(
            shaped(eights(2 * strip), lanes),
            shaped(eights(width * (cols + HALO)), lanes),
        ),
        in_specs=[VMEM] * 3 + [ANY],
        out_specs=(VMEM, VMEM),
        name="relay",
        compiler_params=grant(2),
        cost_estimate=takes(0.5),
    )(edges, message, got, table)
    other = lax.ppermute(relay, "gx", partner)
    first_got = lax.ppermute(first, axes, first_swap)
    inner_got = lax.ppermute(inner, "gx", partner)

    ring = pl.pallas_call(
        functools.partial(join_kernel, cols, width),
        out_shape=shaped(run * strip, lanes),
        in_specs=[VMEM] * 3 + [ANY],
        out_specs=VMEM,
        name="join",
        compiler_params=grant(2),
        cost_estimate=takes(0.5),
    )(message, got, other, relay)
    while run < held:
        shift = run
        more = lax.ppermute(ring, "gx", [((i + shift) % count, i) for i in range(count)])
        ring = jnp.concatenate([ring, more])
        run *= 2

    z_rows = eights(width * (cols + 2 * HALO))
    second = pl.pallas_call(
        functools.partial(rows_kernel, cols, width, count, ends, run),
        out_shape=shaped(z_rows, lanes),
        in_specs=[VMEM] * 5,
        out_specs=VMEM,
        name="rows",
        cost_estimate=takes(1.0),
        compiler_params=grant(2 * pl.cdiv(run, 8)),
    )(table, edges, other, got, ring)
    second_got = lax.ppermute(second, axes, second_swap)

    bands = [band_of(block, second) for block in range(x_blocks)]

    turned, glued, mask = pl.pallas_call(
        functools.partial(turn_kernel, levels, cols, width, count, ends, run),
        out_shape=(shaped(eights(width * HALO), lanes), shaped(z_rows, lanes), shaped(z_rows, lanes)),
        in_specs=[VMEM] + [ANY] * len(bands[:1]) + [VMEM] * 2,
        out_specs=(VMEM, VMEM, VMEM),
        name="turn",
        compiler_params=grant(2),
        cost_estimate=takes(0.1),
    )(first_got, *bands[:1], ring, table)
    turned_got = lax.ppermute(turned, "gx", partner)
    inside = [(x, y) for y in range(1, y_blocks - 1) for x in range(x_blocks)]
    block_shape = (BLOCK_X, BLOCK_Y * levels, lanes)
    middle = pl.pallas_call(
        functools.partial(middle_kernel, levels, inside),
        out_shape=(field_shape, shaped(len(inside), *block_shape)),
        in_specs=[VMEM, VMEM, ANY] + [VMEM] * (1 + x_blocks),
        out_specs=(VMEM, VMEM),
        input_output_aliases={3: 0},
        name="middle",
        cost_estimate=takes(0.7),
        compiler_params=grant(6),
    )
    field, done = middle(inner_got, outer_got, second, field, *bands)
    out_shape = shaped(cols, rows * levels, lanes)
    field, near = pl.pallas_call(
        functools.partial(near_kernel, levels, cols, rows * levels),
        out_shape=(field_shape, shaped(x_blocks, *block_shape)),
        in_specs=[VMEM] * (3 + x_blocks),
        out_specs=(VMEM, VMEM),
        input_output_aliases={2: 0},
        name="near",
        cost_estimate=takes(0.5),
        compiler_params=grant(6),
    )(first_got, turned_got, field, *bands)
    _, updated = pl.pallas_call(
        functools.partial(edge_kernel, levels, cols, rows * levels, inside),
        out_shape=(field_shape, out_shape),
        in_specs=[VMEM] * (7 + x_blocks),
        out_specs=(VMEM, HBM),
        scratch_shapes=[
            pltpu.VMEM((x_blocks, *block_shape), F32),
            pltpu.SemaphoreType.DMA((2 * x_blocks + len(inside),)),
        ],
        input_output_aliases={6: 0},
        name="edge",
        cost_estimate=takes(1.0),
        compiler_params=grant(6),
    )(table, second_got, glued, mask, near, done, field, *bands)
    return updated.reshape(cols, rows, levels, lanes)


def solution(mesh):
    split = P("gx", "gy", None, None)
    in_specs = (split, P("gx", "gy", None), P("gx", "gy", None), P(), P(), P())


    def run(tracers, weights, offsets, owner, codes):
        matrix = jnp.asarray(spread_matrix(tracers.shape[2]), BF16)
        body = jax.shard_map(
            on_device, mesh=mesh, in_specs=in_specs, out_specs=split, check_vma=False
        )
        return body(tracers, weights, offsets, owner, codes, matrix)

    return run
```

```python
import functools

import jax
import jax.numpy as jnp
import numpy as np
from jax import lax
from jax.experimental import pallas as pl
from jax.experimental.pallas import tpu as pltpu
from jax.sharding import PartitionSpec as P

HALO = 3
BLOCK_X = 4
BLOCK_Y = 16
PITCH = 24
LANES = 128
LEAD = 4
BF16 = jnp.bfloat16
F32 = jnp.float32

STENCILS = [
    {(0, 0): 1.0},
    {(1, 0): 0.5, (-1, 0): -0.5},
    {(0, 1): 0.5, (0, -1): -0.5},
    {(1, 0): 0.5, (0, 0): -1.0, (-1, 0): 0.5},
    {(0, 1): 0.5, (0, 0): -1.0, (0, -1): 0.5},
    {(1, 1): 0.25, (1, -1): -0.25, (-1, 1): -0.25, (-1, -1): 0.25},
]


def spread_matrix(levels):
    terms = 24 * levels
    rows = 2 * terms + 8 * pl.cdiv(2 * levels, 8)
    matrix = np.zeros((rows, 2 * levels * LANES), np.float32)
    for level in range(levels):
        for piece in range(4):
            for moment, stencil in enumerate(STENCILS):
                for (east, north), value in stencil.items():
                    lane = (piece // 2 + 1 + east) * PITCH + piece % 2 + 1 + north
                    row = 24 * level + 6 * piece + moment
                    matrix[row, level * LANES + lane] += value
                    matrix[terms + row, level * LANES + lane] += value
        first = (levels + level) * LANES
        matrix[2 * terms + 2 * level, first : first + LANES] = PITCH
        matrix[2 * terms + 2 * level + 1, first : first + LANES] = 1
    return matrix


def load_kernel(count, ends, run, turns, owner_ref, codes_ref, cells_ref, weights_ref, offsets_ref,
                matrix_ref, after_ref, *refs):
    del after_ref
    table_ref, inner_ref, weights_out, offsets_out, matrix_out, field_ref, owner, codes, sems = refs[-9:]

    @pl.when(((lax.axis_index("gx") + 1) // 2 % 2 == 0) == turns)
    def _():
        index, place = lax.axis_index("gx"), lax.axis_index("gy")
        cols, rows, _ = cells_ref.shape
        lead = LEAD * (weights_ref.shape[1] // 24)
        last = cols - HALO
        pairs = [
            (owner_ref, owner),
            (codes_ref, codes),
            (cells_ref.at[pl.ds(jnp.where(index % 2 == 0, last, 0), HALO)], inner_ref),
            (weights_ref, weights_out),
            (offsets_ref, offsets_out),
            (matrix_ref, matrix_out),
        ]
        for col in range(0, cols, BLOCK_X):
            to = field_ref.at[pl.ds(HALO + col, BLOCK_X), pl.ds(lead, rows)]
            pairs.append((cells_ref.at[pl.ds(col, BLOCK_X)], to))
        copies = [pltpu.make_async_copy(a, b, sems.at[at]) for at, (a, b) in enumerate(pairs)]
        for copy in copies:
            copy.start()
        copies[0].wait()
        copies[1].wait()
        side = jnp.where(place == 0, 0, 1)
        window = Window(cells_ref.shape[0], 0, count, run, None)
        target = lax.rem(index + count // 2, count)
        is_end = jnp.logical_or(place == 0, place == ends - 1)
        code = jnp.where(is_end, codes[side, index], 0)
        lines = [window.start(owner[side, target]), window.start(owner[side, index]), code]
        for at, line in enumerate(lines):
            table_ref[at : at + 1] = jnp.full((1, LANES), line, jnp.int32)
        for copy in copies[2:]:
            copy.wait()


def band_kernel(levels, rows, block, weights_ref, offsets_ref, matrix_ref, after_ref, band_ref):
    del after_ref
    y_blocks = rows // BLOCK_Y
    lane = lax.broadcasted_iota(jnp.int32, (rows, LANES), 1)
    row_in = lax.broadcasted_iota(jnp.int32, (rows, LANES), 0) % BLOCK_Y
    base = lane - row_in - 2 * PITCH - 2
    pad = matrix_ref.shape[0] - 2 * weights_ref.shape[1] - offsets_ref.shape[1]

    def column(x):
        weights = weights_ref[x]
        high = weights.astype(BF16).astype(F32)
        stacked = jnp.concatenate(
            [high, weights - high, offsets_ref[x].astype(F32), jnp.zeros((pad, rows), F32)], axis=0
        ).astype(BF16)
        spread = lax.dot_general(
            stacked, matrix_ref[...], (((0,), (0,)), ((), ())), preferred_element_type=F32
        )
        inner = x % BLOCK_X
        at = inner * BLOCK_Y
        low = at + BLOCK_X * BLOCK_Y
        for level in range(levels):
            points = spread[:, level * LANES : (level + 1) * LANES]
            first = (levels + level) * LANES
            shift = spread[:, first : first + LANES].astype(jnp.int32)
            for y in range(y_blocks):
                mine = slice(y * BLOCK_Y, (y + 1) * BLOCK_Y)
                index = base[mine] - shift[mine] - inner * PITCH
                picked = jnp.take_along_axis(
                    points[mine], index & (LANES - 1), axis=1, mode="promise_in_bounds"
                )
                top = picked.astype(BF16).astype(F32)
                rest = picked - top
                here = index >= 0
                slot = y * levels + level
                for part in range(2):
                    lanes = slice(part * LANES, (part + 1) * LANES)
                    keep = here if part == 0 else jnp.logical_not(here)
                    band_ref[slot, at : at + BLOCK_Y, lanes] = jnp.where(keep, top, 0.0).astype(BF16)
                    band_ref[slot, low : low + BLOCK_Y, lanes] = jnp.where(keep, rest, 0.0).astype(BF16)

    for step in range(BLOCK_X):
        column(block * BLOCK_X + step)


def pack_kernel(ends, cells_ref, edges_ref, message_ref, outer_ref, low_ref, high_ref, sems):
    cols, rows, _ = cells_ref.shape
    width = edges_ref.shape[0] // cols // 2
    deep = low_ref.shape[1]
    even, place = lax.axis_index("gx") % 2 == 0, lax.axis_index("gy")
    low, up = place == 0, place % 2 == 0
    is_end = jnp.logical_or(low, place == ends - 1)
    last = cols - HALO
    copies = [
        pltpu.make_async_copy(cells_ref.at[:, pl.ds(0, deep)], low_ref, sems.at[0]),
        pltpu.make_async_copy(cells_ref.at[:, pl.ds(rows - deep, deep)], high_ref, sems.at[1]),
        pltpu.make_async_copy(
            cells_ref.at[pl.ds(jnp.where(even, 0, last), HALO)], outer_ref, sems.at[2]
        ),
    ]
    for copy in copies:
        copy.start()
    for copy in copies[:2]:
        copy.wait()
    for col in range(cols):
        at = 2 * width * col
        bottom, top = low_ref[col, :width], high_ref[col, deep - width :]
        edges_ref[at : at + width] = bottom
        edges_ref[at + width : at + 2 * width] = top
        strip = jnp.where(low, bottom, top)
        if col < HALO:
            bottom = jnp.where(even, bottom, low_ref[last + col, :width])
            top = jnp.where(even, top, high_ref[last + col, deep - width :])
            message_ref[width * col : width * (col + 1)] = jnp.where(up, top, bottom)
            strip = jnp.where(is_end, strip, jnp.where(up, bottom, top))
        to = width * (HALO + col)
        message_ref[to : to + width] = strip
    clear(message_ref, width * (HALO + cols))
    copies[2].wait()


def clear(ref, at):
    if at < ref.shape[0]:
        ref[at:] = jnp.zeros((ref.shape[0] - at, LANES), F32)


def relay_kernel(cols, width, ends, edges_ref, message_ref, got_ref, after_ref, relay_ref,
                 first_ref):
    del after_ref
    even, place = lax.axis_index("gx") % 2 == 0, lax.axis_index("gy")
    up = place % 2 == 0
    is_end = jnp.logical_or(place == 0, place == ends - 1)
    corner, strip = width * HALO, width * cols
    relay_ref[:strip] = message_ref[corner : corner + strip]
    relay_ref[strip : 2 * strip] = got_ref[corner : corner + strip]
    for col in range(HALO):
        left, right = 2 * width * col, 2 * width * (cols - HALO + col)
        low = jnp.where(even, edges_ref[right : right + width], edges_ref[left : left + width])
        left, right = left + width, right + width
        high = jnp.where(even, edges_ref[right : right + width], edges_ref[left : left + width])
        to = slice(width * col, width * (col + 1))
        relay_ref[to] = jnp.where(is_end, relay_ref[to], jnp.where(up, low, high))
    clear(relay_ref, 2 * strip)
    first_ref[:corner] = got_ref[:corner]
    for col in range(cols):
        at = 2 * width * col
        to = corner + width * col
        first_ref[to : to + width] = jnp.where(
            up, edges_ref[at + width : at + 2 * width], edges_ref[at : at + width]
        )
    clear(first_ref, corner + strip)


def turn_kernel(levels, cols, width, count, ends, run, first_ref, *refs):
    run_ref, table_ref, corner_ref, glued_ref, mask_ref = refs[-5:]
    even, place = lax.axis_index("gx") % 2 == 0, lax.axis_index("gy")
    size = HALO * width
    last = (HALO + cols) * width
    corner_ref[:size] = jnp.where(even, first_ref[last - size : last], first_ref[size : 2 * size])
    clear(corner_ref, size)
    wide = cols + 2 * HALO
    window = Window(cols, width, count, run, run_ref)
    start, code = table_ref[1:2, 0:1][0, 0], table_ref[2:3, 0:1][0, 0]
    is_end = jnp.logical_or(place == 0, place == ends - 1)
    mirrored, flipped = code % 2 == 1, code // 2 % 2 == 1
    for u in range(wide):
        to = slice(width * u, width * (u + 1))
        held, strip = window.column(start, jnp.where(mirrored, wide - 1 - u, u))
        glued_ref[to] = jnp.where(flipped, turn_rows(strip, levels), strip)
        mask_ref[to] = jnp.full(
            (width, LANES), jnp.where(jnp.logical_and(is_end, held), 1.0, 0.0), F32
        )
    clear(glued_ref, wide * width)
    clear(mask_ref, wide * width)


def turn_rows(strip, levels):
    return jnp.concatenate(
        [strip[levels * r : levels * (r + 1)] for r in reversed(range(HALO))], axis=0
    )


def join_kernel(cols, width, message_ref, got_ref, other_ref, after_ref, run_ref):
    del after_ref
    even = lax.axis_index("gx") % 2 == 0
    corner, strip = width * HALO, width * cols
    mine, far = message_ref[corner : corner + strip], got_ref[corner : corner + strip]
    near, beyond = other_ref[:strip], other_ref[strip : 2 * strip]
    pairs = ((far, beyond), (mine, near), (near, mine), (beyond, far))
    for at, (a, b) in enumerate(pairs):
        run_ref[at * strip : (at + 1) * strip] = jnp.where(even, a, b)


class Window:
    def __init__(self, cols, width, count, run, held):
        self.cols, self.width, self.total, self.run = cols, width, count * cols, run
        self.held = held
        index = lax.axis_index("gx")
        self.first = index - index % 2 - 1

    def start(self, owner):
        return lax.rem((owner - self.first) * self.cols - HALO + 2 * self.total, self.total)

    def column(self, start, step):
        at = start + step
        at = jnp.where(at >= self.total, at - self.total, at)
        row = jnp.minimum(at, self.run * self.cols - 1) * self.width
        return at < self.run * self.cols, self.held[pl.ds(row, self.width)]


def rows_kernel(cols, width, count, ends, run, table_ref, edges_ref, other_ref, got_ref, run_ref,
                second_ref):
    even, place = lax.axis_index("gx") % 2 == 0, lax.axis_index("gy")
    top = place % 2 == 1

    def column(u):
        if HALO <= u < HALO + cols:
            at = 2 * width * (u - HALO)
            return jnp.where(
                top, edges_ref[at + width : at + 2 * width], edges_ref[at : at + width]
            )
        col = u if u < HALO else u - HALO - cols
        near = other_ref[width * col : width * (col + 1)]
        far = got_ref[width * (HALO + col) : width * (HALO + col + 1)]
        return jnp.where(even == (u < HALO), far, near)

    wide = cols + 2 * HALO
    window = Window(cols, width, count, run, run_ref)
    start = table_ref[0:1, 0:1][0, 0]
    is_end = jnp.logical_or(place == 0, place == ends - 1)
    for u in range(wide):
        to = slice(u * width, (u + 1) * width)
        _, glued = window.column(start, u)
        second_ref[to] = jnp.where(is_end, glued, column(u))
    clear(second_ref, wide * width)


def block_sum(field_ref, bands, x, y, levels, level):
    size = BLOCK_X * BLOCK_Y
    reach = BLOCK_X + 2 * HALO
    begin = (y * BLOCK_Y + LEAD - HALO) * levels + level
    points = jnp.concatenate(
        [
            field_ref[x * BLOCK_X + c, pl.ds(begin, PITCH, stride=levels), :]
            for c in range(reach)
        ]
        + [jnp.zeros((2 * LANES - reach * PITCH, LANES), F32)],
        axis=0,
    )
    top = points.astype(BF16)
    rest = (points - top.astype(F32)).astype(BF16)
    band = bands[x][y * levels + level]
    product = jnp.dot(band, jnp.concatenate([top, rest], axis=1), preferred_element_type=F32)
    return product[:size, :LANES] + (product[:size, LANES:] + product[size:, :LANES])


def remap_blocks(field_ref, bands, stage_ref, levels, blocks, ready=None):
    for at, (x, y) in enumerate(blocks):
        for level in range(levels):
            total = block_sum(field_ref, bands, x, y, levels, level)
            for c in range(BLOCK_X):
                stage_ref[at, c, pl.ds(level, BLOCK_Y, stride=levels), :] = total[
                    c * BLOCK_Y : (c + 1) * BLOCK_Y
                ]
        if ready is not None:
            ready(at, x, y)


def middle_kernel(levels, blocks, inner_ref, outer_ref, after_ref, field_in, *refs):
    del after_ref, field_in
    *bands, field_ref, stage_ref = refs
    rows, wide = inner_ref.shape[1], field_ref.shape[0]
    lead = LEAD * levels
    even = lax.axis_index("gx") % 2 == 0
    for col in range(HALO):
        inner, outer = inner_ref[col], outer_ref[col]
        field_ref[col, lead : lead + rows] = jnp.where(even, outer, inner)
        field_ref[wide - HALO + col, lead : lead + rows] = jnp.where(even, inner, outer)
    remap_blocks(field_ref, bands, stage_ref, levels, blocks)


def put_block(source, out_ref, sem, x, y):
    _, deep, _ = source.shape
    to = out_ref.at[pl.ds(x * BLOCK_X, BLOCK_X), pl.ds(pl.multiple_of(y * deep, deep), deep)]
    copy = pltpu.make_async_copy(source, to, sem)
    copy.start()
    return copy


def near_kernel(levels, cols, rows, first_ref, corner_ref, field_in, *refs):
    del field_in
    *bands, field_ref, stage_ref = refs
    width, lead = HALO * levels, LEAD * levels
    even, up = lax.axis_index("gx") % 2 == 0, lax.axis_index("gy") % 2 == 0
    tail = field_ref.shape[1] - lead - rows - width
    for u in range(cols + 2 * HALO):
        if HALO <= u < HALO + cols:
            strip = first_ref[u * width : (u + 1) * width]
        else:
            col = u if u < HALO else u - HALO - cols
            far = first_ref[col * width : (col + 1) * width]
            near = corner_ref[col * width : (col + 1) * width]
            strip = jnp.where(even == (u < HALO), far, near)
        field_ref[u, lead - width : lead] = strip
        field_ref[u, lead + rows : lead + rows + width] = strip
        field_ref[u, lead + rows + width :] = jnp.zeros((tail, LANES), F32)
    last = rows // levels // BLOCK_Y - 1
    blocks = [(x, jnp.where(up, last, 0)) for x in range(cols // BLOCK_X)]
    remap_blocks(field_ref, bands, stage_ref, levels, blocks)


def edge_kernel(levels, cols, rows, done, table_ref, second_ref, glued_ref, mask_ref, near_ref,
                done_ref, field_in, *refs):
    del field_in
    *bands, field_ref, out_ref, stage_ref, sems = refs
    last = rows // levels // BLOCK_Y - 1
    up = lax.axis_index("gy") % 2 == 0
    blocks = [(x, jnp.where(up, 0, last)) for x in range(cols // BLOCK_X)]
    copies = []
    ready = [(done_ref.at[at], x, y) for at, (x, y) in enumerate(done)]
    ready += [(near_ref.at[x], x, last - y) for x, y in blocks]

    def put(at, x, y):
        copies.append(put_block(stage_ref.at[at], out_ref, sems.at[len(copies)], x, y))

    width, lead = HALO * levels, LEAD * levels
    wide = cols + 2 * HALO
    facing = jnp.where(up, lead - width, lead + rows)
    code = table_ref[2:3, 0:1][0, 0]
    mirrored, flipped = code % 2 == 1, code // 2 % 2 == 1
    for u in range(wide):
        to = slice(width * u, width * (u + 1))
        back = slice(width * (wide - 1 - u), width * (wide - u))
        come = jnp.where(mirrored, second_ref[back], second_ref[to])
        come = jnp.where(flipped, turn_rows(come, levels), come)
        strip = jnp.where(mask_ref[to] > 0, glued_ref[to], come)
        field_ref[u, pl.ds(facing, width)] = strip

    for source, x, y in ready:
        copies.append(put_block(source, out_ref, sems.at[len(copies)], x, y))

    remap_blocks(field_ref, bands, stage_ref, levels, blocks, put)
    for copy in copies:
        copy.wait()


def grant(mebibytes):
    return pltpu.CompilerParams(vmem_limit_bytes=mebibytes << 20)


def takes(microseconds):
    return pl.CostEstimate(
        flops=0, bytes_accessed=int(microseconds * 3_000_000), transcendentals=0
    )


def in_hbm(array):
    return pltpu.with_memory_space_constraint(array, pltpu.HBM)


VMEM = pl.BlockSpec(memory_space=pltpu.VMEM)
HBM = pl.BlockSpec(memory_space=pltpu.HBM)
ANY = pl.BlockSpec(memory_space=pl.ANY)
SMEM = pl.BlockSpec(memory_space=pltpu.SMEM)


def shaped(*shape, dtype=F32):
    return jax.ShapeDtypeStruct(shape, dtype)


def eights(rows):
    return 8 * pl.cdiv(rows, 8)


def on_device(tracers, weights, offsets, owner, codes, matrix):
    cols, rows, levels, lanes = tracers.shape
    width = HALO * levels
    count, ends = lax.axis_size("gx"), lax.axis_size("gy")
    axes = ("gx", "gy")
    cells = tracers.reshape(cols, rows * levels, lanes)
    partner = [(i, i ^ 1) for i in range(count)]
    across = [(i, (i + 1) % count if i % 2 else (i - 1) % count) for i in range(count)]
    first_swap = [(i * ends + j, i * ends + (j ^ 1)) for i in range(count) for j in range(ends)]
    second_swap = []
    for i in range(count):
        for j in range(ends):
            if j in (0, ends - 1):
                second_swap.append((i * ends + j, (i + count // 2) % count * ends + j))
            else:
                second_swap.append((i * ends + j, i * ends + (j + 1 if j % 2 else j - 1)))

    deep = eights(width)
    strip, corner = width * cols, width * HALO
    columns = shaped(HALO, rows * levels, lanes)
    edges, message, outer = pl.pallas_call(
        functools.partial(pack_kernel, ends),
        out_shape=(shaped(2 * strip, lanes), shaped(eights(strip + corner), lanes), columns),
        in_specs=[HBM],
        out_specs=(VMEM, VMEM, VMEM),
        scratch_shapes=[
            pltpu.VMEM((cols, deep, lanes), F32),
            pltpu.VMEM((cols, deep, lanes), F32),
            pltpu.SemaphoreType.DMA((3,)),
        ],
        name="pack",
        compiler_params=grant(4),
        cost_estimate=takes(1.0),
    )(in_hbm(cells))
    got = lax.ppermute(message, "gx", across)
    outer_got = lax.ppermute(outer, "gx", across)

    field_rows = eights((LEAD + rows + HALO + PITCH - BLOCK_Y - 2 * HALO) * levels)
    field_shape = shaped(cols + 2 * HALO, field_rows, lanes)
    run = 4
    held = max(run, count // 2)
    weights = jnp.swapaxes(weights, 1, 2)
    offsets = jnp.swapaxes(offsets, 1, 2)
    loaded = (
        shaped(8, lanes, dtype=jnp.int32),
        columns,
        shaped(*weights.shape),
        shaped(*offsets.shape, dtype=jnp.int32),
        shaped(*matrix.shape, dtype=BF16),
        field_shape,
    )
    sources = [in_hbm(a) for a in (owner, codes, cells, weights, offsets, matrix)] + [message]

    def load(turns, into):
        return pl.pallas_call(
            functools.partial(load_kernel, count, ends, held, turns),
            out_shape=loaded,
            in_specs=[HBM] * 6 + [ANY] + [VMEM] * len(into),
            out_specs=(VMEM,) * 6,
            scratch_shapes=[
                pltpu.SMEM(owner.shape, jnp.int32),
                pltpu.SMEM(codes.shape, jnp.int32),
                pltpu.SemaphoreType.DMA((6 + cols // BLOCK_X,)),
            ],
            input_output_aliases={7 + at: at for at in range(len(into))},
            name="load",
            compiler_params=grant(6),
            cost_estimate=takes(0.5),
        )(*sources, *into)

    parts = load(False, ())
    table, inner, weights, offsets, matrix, field = load(True, parts)

    x_blocks, y_blocks = cols // BLOCK_X, rows // BLOCK_Y

    def band_of(block, after):
        return pl.pallas_call(
            functools.partial(band_kernel, levels, rows, block),
            out_shape=shaped(y_blocks * levels, 2 * BLOCK_X * BLOCK_Y, 2 * LANES, dtype=BF16),
            in_specs=[VMEM] * 3 + [ANY],
            out_specs=VMEM,
            name="band",
            compiler_params=grant(4),
            cost_estimate=takes(0.5),
        )(weights, offsets, matrix, after)

    relay, first = pl.pallas_call(
        functools.partial(relay_kernel, cols, width, ends),
        out_shape=(
            shaped(eights(2 * strip), lanes),
            shaped(eights(width * (cols + HALO)), lanes),
        ),
        in_specs=[VMEM] * 3 + [ANY],
        out_specs=(VMEM, VMEM),
        name="relay",
        compiler_params=grant(2),
        cost_estimate=takes(0.5),
    )(edges, message, got, table)
    other = lax.ppermute(relay, "gx", partner)
    first_got = lax.ppermute(first, axes, first_swap)
    inner_got = lax.ppermute(inner, "gx", partner)

    ring = pl.pallas_call(
        functools.partial(join_kernel, cols, width),
        out_shape=shaped(run * strip, lanes),
        in_specs=[VMEM] * 3 + [ANY],
        out_specs=VMEM,
        name="join",
        compiler_params=grant(2),
        cost_estimate=takes(0.5),
    )(message, got, other, relay)
    while run < held:
        shift = run
        more = lax.ppermute(ring, "gx", [((i + shift) % count, i) for i in range(count)])
        ring = jnp.concatenate([ring, more])
        run *= 2

    z_rows = eights(width * (cols + 2 * HALO))
    second = pl.pallas_call(
        functools.partial(rows_kernel, cols, width, count, ends, run),
        out_shape=shaped(z_rows, lanes),
        in_specs=[VMEM] * 5,
        out_specs=VMEM,
        name="rows",
        cost_estimate=takes(1.0),
        compiler_params=grant(2 * pl.cdiv(run, 8)),
    )(table, edges, other, got, ring)
    second_got = lax.ppermute(second, axes, second_swap)

    bands = [band_of(block, second) for block in range(x_blocks)]

    turned, glued, mask = pl.pallas_call(
        functools.partial(turn_kernel, levels, cols, width, count, ends, run),
        out_shape=(shaped(eights(width * HALO), lanes), shaped(z_rows, lanes), shaped(z_rows, lanes)),
        in_specs=[VMEM] + [ANY] * len(bands[:2]) + [VMEM] * 2,
        out_specs=(VMEM, VMEM, VMEM),
        name="turn",
        compiler_params=grant(2),
        cost_estimate=takes(0.1),
    )(first_got, *bands[:2], ring, table)
    turned_got = lax.ppermute(turned, "gx", partner)
    inside = [(x, y) for y in range(1, y_blocks - 1) for x in range(x_blocks)]
    block_shape = (BLOCK_X, BLOCK_Y * levels, lanes)
    middle = pl.pallas_call(
        functools.partial(middle_kernel, levels, inside),
        out_shape=(field_shape, shaped(len(inside), *block_shape)),
        in_specs=[VMEM, VMEM, ANY] + [VMEM] * (1 + x_blocks),
        out_specs=(VMEM, VMEM),
        input_output_aliases={3: 0},
        name="middle",
        cost_estimate=takes(0.7),
        compiler_params=grant(6),
    )
    field, done = middle(inner_got, outer_got, second, field, *bands)
    out_shape = shaped(cols, rows * levels, lanes)
    field, near = pl.pallas_call(
        functools.partial(near_kernel, levels, cols, rows * levels),
        out_shape=(field_shape, shaped(x_blocks, *block_shape)),
        in_specs=[VMEM] * (3 + x_blocks),
        out_specs=(VMEM, VMEM),
        input_output_aliases={2: 0},
        name="near",
        cost_estimate=takes(0.5),
        compiler_params=grant(6),
    )(first_got, turned_got, field, *bands)
    _, updated = pl.pallas_call(
        functools.partial(edge_kernel, levels, cols, rows * levels, inside),
        out_shape=(field_shape, out_shape),
        in_specs=[VMEM] * (7 + x_blocks),
        out_specs=(VMEM, HBM),
        scratch_shapes=[
            pltpu.VMEM((x_blocks, *block_shape), F32),
            pltpu.SemaphoreType.DMA((2 * x_blocks + len(inside),)),
        ],
        input_output_aliases={6: 0},
        name="edge",
        cost_estimate=takes(1.0),
        compiler_params=grant(6),
    )(table, second_got, glued, mask, near, done, field, *bands)
    return updated.reshape(cols, rows, levels, lanes)


def solution(mesh):
    split = P("gx", "gy", None, None)
    in_specs = (split, P("gx", "gy", None), P("gx", "gy", None), P(), P(), P())


    def run(tracers, weights, offsets, owner, codes):
        matrix = jnp.asarray(spread_matrix(tracers.shape[2]), BF16)
        body = jax.shard_map(
            on_device, mesh=mesh, in_specs=in_specs, out_specs=split, check_vma=False
        )
        return body(tracers, weights, offsets, owner, codes, matrix)

    return run
```
